32 devices in a mesh: rows: 16 (over z, x, core), win: 2 (over y).
Axes of the slice: x: 2, y: 2, z: 4, core: 2. Of those that a mesh axis runs over, the one named last changes fastest.
Arguments:
- table: bfloat16 [2048, 16, 256], P(('win', 'rows')), parts along dimension 0, may hold values from -6 to 6
- row_mask: int32 [2048], P(('win', 'rows')), parts along dimension 0, may hold values from 0 to 1, as said below
- column_types: int32 [32], P('win'), parts along dimension 0, may hold values from 0 to 7
- type_table: bfloat16 [8, 256], replicated, may hold values from -4 to 4
- row_inputs: bfloat16 [256, 768], replicated, may hold values from -0.375 to 0.375
- row_merge: bfloat16 [256, 256], replicated, may hold values from -0.375 to 0.375
- column_inputs: bfloat16 [256, 768], replicated, may hold values from -0.375 to 0.375
- column_merge: bfloat16 [256, 256], replicated, may hold values from -0.375 to 0.375
- summary_queries: bfloat16 [256, 256], replicated, may hold values from -1 to 1
- summary_pairs: bfloat16 [256, 512], replicated, may hold values from -0.375 to 0.375
- summary_merge: bfloat16 [256, 256], replicated, may hold values from -0.375 to 0.375
- expand_weight: bfloat16 [256, 512], replicated, may hold values from -0.375 to 0.375
- reduce_weight: bfloat16 [512, 256], replicated, may hold values from -0.25 to 0.25
- out_cotangent: bfloat16 [2048, 16, 256], P(('win', 'rows')), parts along dimension 0, may hold values from -6 to 6
Outputs:
- encoded: bfloat16 [2048, 16, 256], P(('win', 'rows')), parts along dimension 0
- table_grad: bfloat16 [2048, 16, 256], P(('win', 'rows')), parts along dimension 0
- type_table_grad: float32 [16, 256], P('win'), parts along dimension 0
- row_inputs_grad: float32 [512, 768], P('win'), parts along dimension 0
- row_merge_grad: float32 [512, 256], P('win'), parts along dimension 0
- column_inputs_grad: float32 [512, 768], P('win'), parts along dimension 0
- column_merge_grad: float32 [512, 256], P('win'), parts along dimension 0
- summary_queries_grad: float32 [512, 256], P('win'), parts along dimension 0
- summary_pairs_grad: float32 [512, 512], P('win'), parts along dimension 0
- summary_merge_grad: float32 [512, 256], P('win'), parts along dimension 0
- expand_grad: float32 [512, 512], P('win'), parts along dimension 0
- reduce_grad: float32 [1024, 256], P('win'), parts along dimension 0
The draws below stay inside these ranges and needn't reach their ends.
There are 2 independent parts, one for each index of `win`. The reference program is written for one: setup_inputs(seed, part) draws one part's arguments, and reference() takes and returns one part's arrays. A program takes and returns all parts, laid end to end along the dimension named above; an argument that names none is the same for every part. Nothing has to cross between parts.
Inputs may be any that keep to these rules, and one draw needn't show every extreme that they name: row_mask is 1 on every row except the last rows of the final 64-row span; that span keeps its first 1 to 63 rows valid and the rest are 0.
All inputs are finite; a program needn't handle non-finite values.
Results may differ from the reference program's by a relative error of at most 0.015.
Values may be sent and summed in bfloat16 or wider, within the bound.
A program may use at most 128 MiB of HBM per device.

```python
import math
from functools import partial
import jax
import jax.numpy as jnp
from jax import lax

D = 256
HEADS = 8
FF = 512
COLS = 16
NTYPES = 8
SPAN = 64
ROWS = 1024


def draw_row_mask(key, part):
    valid_tail = jax.random.randint(key, (), 1, SPAN)
    position = jnp.arange(ROWS, dtype=jnp.int32)
    return (position < ROWS - SPAN + valid_tail).astype(jnp.int32)


def plant(values, own_key, low, largest):
    shape = values.shape
    spot = [jax.random.randint(jax.random.fold_in(own_key, axis), (), 0, shape[axis]) for axis in range(len(shape))]
    values = values.at[tuple(spot)].set(low)
    longest = shape.index(max(shape))
    spot[longest] = (spot[longest] + 1) % shape[longest]
    return values.at[tuple(spot)].set(largest)


def block_scale(stream_key, dims, cuts, least, top_value):
    def one(dim, blocks):
        draws = jax.random.uniform(jax.random.fold_in(jax.random.fold_in(stream_key, 6), dim), (blocks,), jnp.float32, least / len(cuts), top_value / len(cuts))
        return jnp.repeat(jnp.exp(draws), dims[dim] // blocks).reshape((-1,) + (1,) * (len(dims) - dim - 1))

    gain = one(*cuts[0])
    for cut in cuts[1:]:
        gain = gain * one(*cut)
    return gain


def gaussian(key, extent, deviation, most, shards=(), kind=jnp.bfloat16):
    level = block_scale(key, extent, shards, -0.22, 0.18) if shards else 1.0
    entries = jax.random.normal(key, extent, jnp.float32) * deviation * level
    return jnp.minimum(jnp.maximum(entries, -most), most).astype(kind)


def setup_inputs(seed: int = 0, part: int = 0) -> dict:
    seeds = jax.random.split(jax.random.key(seed), 15)
    part_splits = jax.random.split(jax.random.fold_in(seeds[14], part), 15)
    table = gaussian(part_splits[0], (ROWS, COLS, D), 1.0, 6.0, ((0, 16),))
    row_mask = draw_row_mask(jax.random.fold_in(jax.random.fold_in(seeds[14], part), 71), part)
    column_types = plant(jax.random.randint(part_splits[2], (COLS,), 0, NTYPES), jax.random.fold_in(part_splits[2], 1), 0, NTYPES - 1).astype(jnp.int32)
    type_table = gaussian(seeds[3], (NTYPES, D), 1.0, 4.0)
    row_inputs = gaussian(seeds[4], (D, 3 * D), D ** -0.5, 0.375)
    row_merge = gaussian(seeds[5], (D, D), D ** -0.5, 0.375)
    column_inputs = gaussian(seeds[6], (D, 3 * D), D ** -0.5, 0.375)
    column_merge = gaussian(seeds[7], (D, D), D ** -0.5, 0.375)
    summary_queries = gaussian(seeds[8], (D, D), (D // 8) ** -0.5, 1.0)
    summary_pairs = gaussian(seeds[9], (D, 2 * D), D ** -0.5, 0.375)
    summary_merge = gaussian(seeds[10], (D, D), D ** -0.5, 0.375)
    expand_weight = gaussian(seeds[11], (D, FF), D ** -0.5, 0.375)
    reduce_weight = gaussian(seeds[12], (FF, D), FF ** -0.5, 0.25)
    out_cotangent = gaussian(part_splits[13], (ROWS, COLS, D), 1.0, 6.0, ((0, 16),))
    return {"table": table, "row_mask": row_mask, "column_types": column_types, "type_table": type_table, "row_inputs": row_inputs, "row_merge": row_merge, "column_inputs": column_inputs, "column_merge": column_merge, "summary_queries": summary_queries, "summary_pairs": summary_pairs, "summary_merge": summary_merge, "expand_weight": expand_weight, "reduce_weight": reduce_weight, "out_cotangent": out_cotangent}


EPSILON = 1e-05

def normalize(values):
    center = values - lax.optimization_barrier(jnp.mean(values, axis=-1, keepdims=True))
    spread = lax.optimization_barrier(jnp.mean(center * center, axis=-1, keepdims=True))
    return center * lax.rsqrt(spread + EPSILON)

def stored(values):
    return lax.optimization_barrier(values.astype(jnp.bfloat16))

def project(active, weight):
    flattened = active.reshape(-1, active.shape[-1])
    result = jnp.dot(flattened, weight, preferred_element_type=jnp.float32)
    return result.reshape(active.shape[:-1] + (weight.shape[1],))

def split_heads(values, head_count):
    return values.reshape(values.shape[:-1] + (head_count, values.shape[-1] // head_count))

def row_attention(row_qkv, head_count):
    width = row_qkv.shape[-1] // 3
    query = split_heads(row_qkv[..., :width].astype(jnp.float32), head_count)
    keys = split_heads(row_qkv[..., width:2 * width].astype(jnp.float32), head_count)
    values = split_heads(row_qkv[..., 2 * width:].astype(jnp.float32), head_count)
    factor = 1.0 / math.sqrt(query.shape[-1])
    scores = jnp.exp(jnp.einsum('rqhe,rkhe->rhqk', query, keys) * factor)
    shares = stored(scores / lax.optimization_barrier(jnp.sum(scores, axis=-1, keepdims=True)))
    mixed = jnp.einsum('rhqk,rkhe->rqhe', shares.astype(jnp.float32), values)
    return mixed.reshape(row_qkv.shape[:-1] + (width,)).astype(jnp.bfloat16)

def row_layer(row_qkv, head_count, steps):
    attend = jax.checkpoint(partial(row_attention, head_count=head_count))
    if steps == 1:
        return attend(row_qkv)
    blocks = row_qkv.reshape((steps, row_qkv.shape[0] // steps) + row_qkv.shape[1:])
    mixed = lax.map(attend, blocks)
    return mixed.reshape(row_qkv.shape[:-1] + (row_qkv.shape[-1] // 3,))

def column_attention(query, current, previous, mask_now, mask_before, head_count):
    width = query.shape[-1]
    window = jnp.concatenate([previous, current], axis=1)
    allowed = jnp.concatenate([mask_before, mask_now], axis=1)
    query_heads = split_heads(query, head_count)
    key_heads = split_heads(window[..., :width], head_count)
    value_heads = split_heads(window[..., width:], head_count)
    factor = 1.0 / math.sqrt(query_heads.shape[-1])
    scores = jnp.exp(jnp.einsum('bqche,bkche->bchqk', query_heads, key_heads) * factor)
    scores = scores * allowed[:, None, None, None, :]
    shares = stored(scores / lax.optimization_barrier(jnp.sum(scores, axis=-1, keepdims=True)))
    mixed = jnp.einsum('bchqk,bkche->bqche', shares.astype(jnp.float32), value_heads)
    return mixed.reshape(query.shape).astype(jnp.bfloat16)

def column_layer(qkv_float, halo, validity, halo_valid, head_count, half_rows, steps):
    row_count, column_count, triple = qkv_float.shape
    width = triple // 3
    blocks = row_count // half_rows
    query = qkv_float[..., :width].reshape(blocks, half_rows, column_count, width)
    current = qkv_float[..., width:].reshape(blocks, half_rows, column_count, 2 * width)
    previous = jnp.concatenate([halo, qkv_float[:row_count - half_rows, :, width:]], axis=0)
    previous = previous.reshape(blocks, half_rows, column_count, 2 * width)
    mask_now = validity.reshape(blocks, half_rows)
    mask_before = jnp.concatenate([halo_valid, validity[:row_count - half_rows]]).reshape(blocks, half_rows)
    attend = jax.checkpoint(partial(column_attention, head_count=head_count))
    if steps == 1:
        mixed = attend(query, current, previous, mask_now, mask_before)
    else:
        group = blocks // steps
        pieces = tuple((piece.reshape((steps, group) + piece.shape[1:]) for piece in (query, current, previous, mask_now, mask_before)))
        mixed = lax.map(lambda items: attend(items[0], items[1], items[2], items[3], items[4]), pieces)
    return mixed.reshape(row_count, column_count, width)

def summarize(after_columns, validity, span_rows):
    row_count, column_count, model_width = after_columns.shape
    groups = row_count // span_rows
    weights = validity.reshape(groups, span_rows, 1, 1)
    totals = lax.optimization_barrier(jnp.sum(after_columns.reshape(groups, span_rows, column_count, model_width) * weights, axis=1))
    counts = lax.optimization_barrier(jnp.sum(validity.reshape(groups, span_rows), axis=1))
    return (totals / counts[:, None, None]).reshape(groups * column_count, model_width)

def summary_attention(query, pairs, head_count):
    width = query.shape[-1]
    query_heads = split_heads(query, head_count)
    key_heads = split_heads(pairs[:, :width], head_count)
    value_heads = split_heads(pairs[:, width:], head_count)
    factor = 1.0 / math.sqrt(query_heads.shape[-1])
    scores = jnp.exp(jnp.einsum('mhe,nhe->hmn', query_heads, key_heads) * factor)
    shares = stored(scores / lax.optimization_barrier(jnp.sum(scores, axis=-1, keepdims=True)))
    mixed = jnp.einsum('hmn,nhe->mhe', shares.astype(jnp.float32), value_heads)
    return mixed.reshape(query.shape).astype(jnp.bfloat16)

def summary_layer(query, pairs, head_count, steps):
    attend = jax.checkpoint(partial(summary_attention, head_count=head_count))
    if steps == 1:
        return attend(query, pairs)
    blocks = query.reshape(steps, query.shape[0] // steps, query.shape[1])
    mixed = lax.map(lambda block: attend(block, pairs), blocks)
    return mixed.reshape(query.shape)

def first_half(table, type_float, row_inputs, row_merge, column_inputs, selector, mapped):
    row_count = table.shape[0]
    residual = table.astype(jnp.float32) + jnp.dot(selector, type_float, precision=lax.Precision.HIGHEST)[None]
    row_norm = stored(normalize(residual))
    row_qkv = stored(project(row_norm, row_inputs))
    row_mixed = row_layer(row_qkv, HEADS, row_count // SPAN if mapped else 1)
    after_rows = residual + project(row_mixed, row_merge)
    column_norm = stored(normalize(after_rows))
    return (after_rows, stored(project(column_norm, column_inputs)))

def second_half(after_rows, qkv_float, halo, column_merge, validity, halo_valid, mapped):
    row_count = after_rows.shape[0]
    steps = row_count // SPAN if mapped else 1
    column_mixed = column_layer(qkv_float, halo, validity, halo_valid, HEADS, SPAN // 2, steps)
    after_columns = after_rows + project(column_mixed, column_merge)
    return (after_columns, stored(normalize(summarize(after_columns, validity, SPAN))))

def summary_heads(summary_norm, summary_queries, summary_pairs):
    return (stored(project(summary_norm, summary_queries)), stored(project(summary_norm, summary_pairs)))

def finish(after_columns, query_float, pairs_float, summary_merge, expand_weight, reduce_weight, mapped):
    row_count, column_count, model_width = after_columns.shape
    groups = row_count // SPAN
    summary_mixed = summary_layer(query_float, pairs_float, HEADS, groups if mapped else 1)
    span_term = project(summary_mixed, summary_merge).reshape(groups, 1, column_count, model_width)
    mixed_in = (after_columns.reshape(groups, SPAN, column_count, model_width) + span_term).reshape(row_count, column_count, model_width)
    feed_norm = stored(normalize(mixed_in))
    hidden = stored(jax.nn.gelu(project(feed_norm, expand_weight)))
    return (mixed_in + project(hidden, reduce_weight)).astype(jnp.bfloat16)

def reference(table, row_mask, column_types, type_table, row_inputs, row_merge, column_inputs, column_merge, summary_queries, summary_pairs, summary_merge, expand_weight, reduce_weight, out_cotangent):
    validity = row_mask.astype(jnp.float32)
    selector = (column_types[:, None] == jnp.arange(NTYPES, dtype=jnp.int32)[None, :]).astype(jnp.float32)
    params = tuple((weight.astype(jnp.float32) for weight in (type_table, row_inputs, row_merge, column_inputs, column_merge, summary_queries, summary_pairs, summary_merge, expand_weight, reduce_weight)))
    column_count = table.shape[1]
    model_width = table.shape[2]
    halo = jnp.zeros((SPAN // 2, column_count, 2 * model_width), jnp.float32)
    halo_valid = jnp.zeros((SPAN // 2,), jnp.float32)

    def whole(table_in, type_in, row_in, row_out, column_in, column_out, query_in, pair_in, merge_in, expand_in, reduce_in):
        after_rows, column_qkv = first_half(table_in, type_in, row_in, row_out, column_in, selector, True)
        after_columns, summary_norm = second_half(after_rows, column_qkv.astype(jnp.float32), halo, column_out, validity, halo_valid, True)
        summary_query, summary_kv = summary_heads(summary_norm, query_in, pair_in)
        return finish(after_columns, summary_query.astype(jnp.float32), summary_kv.astype(jnp.float32), merge_in, expand_in, reduce_in, True)
    encoded, pullback = jax.vjp(whole, table, *params)
    grads = pullback(out_cotangent)
    factor = 1.0 / math.sqrt(ROWS * COLS)
    return (encoded, grads[0], grads[1] * factor, grads[2] * factor, grads[3] * factor, grads[4] * factor, grads[5] * factor, grads[6] * factor, grads[7] * factor, grads[8] * factor, grads[9] * factor, grads[10] * factor)
```

```python
from functools import partial
import math

import jax
import jax.numpy as jnp
from jax import lax
from jax.experimental import pallas as pl
from jax.experimental.pallas import tpu as pltpu
from jax.sharding import PartitionSpec as P

HEADS = 8
NTYPES = 8
SPAN = 64
EPSILON = 1e-05
F32 = jnp.float32
BF16 = jnp.bfloat16
VMEM_LIMIT = 56 * 1024 * 1024


def from_behind(block, axis, distance):
    devices = range(lax.axis_size(axis))
    route = [(i - distance, i) for i in devices if i - distance in devices]
    return lax.ppermute(block, axis, route)


def dot_nn(a, b):
    return lax.dot_general(a, b, (((1,), (0,)), ((), ())), preferred_element_type=F32)


def dot_nt(a, b):
    return lax.dot_general(a, b, (((1,), (1,)), ((), ())), preferred_element_type=F32)


def dot_tn(a, b):
    return lax.dot_general(a, b, (((0,), (0,)), ((), ())), preferred_element_type=F32)


def norm(x):
    center = x - jnp.mean(x, axis=-1, keepdims=True)
    scale = lax.rsqrt(jnp.mean(center * center, axis=-1, keepdims=True) + EPSILON)
    return center * scale, scale


def norm_back(grad, hat, scale):
    first = jnp.mean(grad, axis=-1, keepdims=True)
    second = jnp.mean(grad * hat, axis=-1, keepdims=True)
    return scale * (grad - first - hat * second)


def stack_heads(x):
    head = lax.broadcasted_iota(jnp.int32, (1, x.shape[1]), 1) // (x.shape[1] // HEADS)
    return jnp.concatenate([x * (head == h).astype(F32).astype(BF16) for h in range(HEADS)], axis=0)


def merge_heads(x):
    n = x.shape[0] // HEADS
    head = lax.broadcasted_iota(jnp.int32, (n, x.shape[1]), 1) // (x.shape[1] // HEADS)
    out = x[:n]
    for h in range(1, HEADS):
        out = jnp.where(head == h, x[h * n : (h + 1) * n], out)
    return out


def shares_of(stacked, keys, allowed):
    width = keys.shape[1] // HEADS
    scores = jnp.exp2(dot_nt(keys, stacked) * (math.log2(math.e) / math.sqrt(width)))
    if allowed is not None:
        scores = jnp.where(allowed, scores, 0.0)
    return scores / jnp.sum(scores, axis=0, keepdims=True)


def attend(query, keys, values, allowed):
    shares = shares_of(stack_heads(query), keys, allowed).astype(BF16)
    return merge_heads(dot_tn(shares, values)).astype(BF16)


def attend_back(query, keys, values, grad, allowed):
    width = keys.shape[1] // HEADS
    stacked = stack_heads(query)
    grads = stack_heads(grad)
    shares = shares_of(stacked, keys, allowed)
    share_grad = dot_nt(values, grads)
    total = jnp.sum(share_grad * shares, axis=0, keepdims=True)
    score_grad = (shares * (share_grad - total) * (1.0 / math.sqrt(width))).astype(BF16)
    query_grad = merge_heads(dot_tn(score_grad, keys))
    key_grad = dot_nn(score_grad, stacked)
    value_grad = dot_nn(shares.astype(BF16), grads)
    return query_grad, key_grad, value_grad


def row_allowed(cells, cols):
    key = lax.broadcasted_iota(jnp.int32, (cells, HEADS * cells), 0)
    query = lax.broadcasted_iota(jnp.int32, (cells, HEADS * cells), 1)
    return key // cols == (query % cells) // cols


def column_allowed(rows, valid):
    half = rows // 2
    shape = (rows + half, HEADS * rows)
    key = lax.broadcasted_iota(jnp.int32, shape, 0)
    start = (lax.broadcasted_iota(jnp.int32, shape, 1) % rows) // half * half
    return (key >= start) & (key < start + rows) & (valid > 0.5)


def first_kernel(table, types, row_in, row_merge, col_in, row_norm, row_qkv, row_mixed, after_rows, col_norm, col_qkv, edge):
    cells = types.shape[0]
    width = types.shape[1]
    groups = table.shape[0] // cells
    allowed = row_allowed(cells, 16)

    def step(g, _):
        at = pl.ds(pl.multiple_of(g * cells, cells), cells)
        residual = table[at, :].astype(F32) + types[...]
        normed = norm(residual)[0].astype(BF16)
        row_norm[at, :] = normed
        qkv = dot_nn(normed, row_in[...]).astype(BF16)
        row_qkv[at, :] = qkv
        mixed = attend(qkv[:, :width], qkv[:, width : 2 * width], qkv[:, 2 * width :], allowed)
        row_mixed[at, :] = mixed
        after = residual + dot_nn(mixed, row_merge[...])
        after_rows[at, :] = after
        cnormed = norm(after)[0].astype(BF16)
        col_norm[at, :] = cnormed
        cqkv = dot_nn(cnormed, col_in[...]).astype(BF16)
        col_qkv[at, :] = cqkv.astype(F32)

        @pl.when(g >= groups // 2)
        def _():
            edge[pl.ds(pl.multiple_of((g - groups // 2) * cells, cells), cells), :] = cqkv[:, width:]

        return 0

    lax.fori_loop(0, groups, step, 0)


def column_parts(cqkv, halo, column, rows, cols, width):
    here = pl.ds(column, rows, stride=cols)
    before = pl.ds(column, rows // 2, stride=cols)
    parts = []
    for i in range(width // 128 * 3):
        parts.append(cqkv[i][here, :].astype(BF16))
    halos = [halo[i][before, :].astype(BF16) for i in range(width // 128 * 2)]
    per = width // 128
    query = jnp.concatenate(parts[:per], axis=1)
    keys = jnp.concatenate([jnp.concatenate(halos[:per], axis=1), jnp.concatenate(parts[per : 2 * per], axis=1)], axis=0)
    values = jnp.concatenate([jnp.concatenate(halos[per:], axis=1), jnp.concatenate(parts[2 * per :], axis=1)], axis=0)
    return query, keys, values


def spread(src, dst):
    for i in range(dst.shape[0]):
        dst[i] = src[:, i * 128 : (i + 1) * 128].astype(F32)


def second_kernel(after_rows, cqkv, halo, valid_keys, weights, col_merge, squeries, spairs, col_mixed, after_columns, summary, summary_norm, squery, skv, cqkv_s, halo_s, mixed_s):
    cells, width = after_rows.shape
    rows = SPAN
    cols = cells // rows
    spread(cqkv, cqkv_s)
    spread(halo, halo_s)
    allowed = column_allowed(rows, valid_keys[...])

    def step(c, _):
        query, keys, values = column_parts([cqkv_s.at[i] for i in range(6)], [halo_s.at[i] for i in range(4)], c, rows, cols, width)
        mixed = attend(query, keys, values, allowed).astype(F32)
        for i in range(width // 128):
            mixed_s.at[i][pl.ds(c, rows, stride=cols), :] = mixed[:, i * 128 : (i + 1) * 128]
        return 0

    lax.fori_loop(0, cols, step, 0)
    chunk = 128
    summary[...] = jnp.zeros_like(summary)

    def merge(g, _):
        at = pl.ds(pl.multiple_of(g * chunk, chunk), chunk)
        mixed = jnp.concatenate([mixed_s.at[i][at, :] for i in range(width // 128)], axis=1).astype(BF16)
        col_mixed[at, :] = mixed
        after = after_rows[at, :] + dot_nn(mixed, col_merge[...])
        after_columns[at, :] = after
        weighted = after * weights[at, :]
        summary[...] += jnp.sum(weighted.reshape(chunk // cols, cols, width), axis=0)
        return 0

    lax.fori_loop(0, cells // chunk, merge, 0)
    normed = norm(summary[...])[0].astype(BF16)
    summary_norm[...] = normed
    squery[...] = dot_nn(normed, squeries[...]).astype(BF16)
    skv[...] = dot_nn(normed, spairs[...]).astype(BF16)


def gelu_parts(x):
    k = math.sqrt(2.0 / math.pi)
    t = jnp.tanh(k * (x + 0.044715 * x * x * x))
    value = 0.5 * x * (1.0 + t)
    slope = 0.5 * (1.0 + t) + 0.5 * x * (1.0 - t * t) * (k * (1.0 + 3 * 0.044715 * x * x))
    return value, slope


def third_kernel(scale, after_columns, squery, pairs, cot, smerge, expand, reduce, encoded, col_grad, query_grad, pair_grad, merge_g, expand_g, reduce_g, span_s, hidden_s, feed_s, du_s):
    cells, width = after_columns.shape
    cols = squery.shape[0]
    query = squery[...]
    keys = pairs[:, :width]
    values = pairs[:, width:]
    mixed = attend(query, keys, values, None)
    chunk = 128
    term = jnp.concatenate([dot_nn(mixed, smerge[...])] * (chunk // cols), axis=0)
    span_s[...] = jnp.zeros_like(span_s)

    def step(g, _):
        at = pl.ds(pl.multiple_of(g * chunk, chunk), chunk)
        mixed_in = after_columns[at, :] + term
        hat, inv = norm(mixed_in)
        feed = hat.astype(BF16)
        value, slope = gelu_parts(dot_nn(feed, expand[...]))
        hidden = value.astype(BF16)
        encoded[at, :] = (mixed_in + dot_nn(hidden, reduce[...])).astype(BF16)
        g_out = cot[at, :]
        d_up = (dot_nt(g_out, reduce[...]) * slope).astype(BF16)
        d_feed = dot_nt(d_up, expand[...])
        d_in = g_out.astype(F32) + norm_back(d_feed, hat, inv)
        col_grad[at, :] = d_in
        span_s[...] += jnp.sum(d_in.reshape(chunk // cols, cols, width), axis=0)
        hidden_s[at, :] = hidden
        feed_s[at, :] = feed
        du_s[at, :] = d_up
        return 0

    lax.fori_loop(0, cells // chunk, step, 0)
    d_span = span_s[...].astype(BF16)
    merge_g[...] = (dot_tn(mixed, d_span) * scale).astype(merge_g.dtype)
    d_mixed = dot_nt(d_span, smerge[...]).astype(BF16)
    dq, dk, dv = attend_back(query, keys, values, d_mixed, None)
    query_grad[...] = dq.astype(BF16)
    pair_grad[:, :width] = dk.astype(pair_grad.dtype)
    pair_grad[:, width:] = dv.astype(pair_grad.dtype)
    expand_g[...] = (dot_tn(feed_s[...], du_s[...]) * scale).astype(expand_g.dtype)
    reduce_g[...] = (dot_tn(hidden_s[...], cot[...]) * scale).astype(reduce_g.dtype)


def fourth_kernel(scale, col_grad, query_grad, pair_share, summary, summary_norm, weights, cqkv, halo, valid_keys, col_mixed, col_merge, squeries, spairs, d_after, dqkv, halo_grad, queries_g, pairs_g, merge_g, cqkv_s, halo_s, dmix_s, dqkv_s, dhalo_s, dab_s):
    cells, width = col_grad.shape
    rows = SPAN
    cols = cells // rows
    spread(cqkv, cqkv_s)
    spread(halo, halo_s)
    qg = query_grad[...]
    pg = pair_share[...].astype(BF16)
    queries_g[...] = (dot_tn(summary_norm[...], qg) * scale).astype(queries_g.dtype)
    pairs_g[...] = (dot_tn(summary_norm[...], pg) * scale).astype(pairs_g.dtype)
    d_norm = dot_nt(qg, squeries[...]) + dot_nt(pg, spairs[...])
    hat, inv = norm(summary[...])
    chunk = 128
    d_summary = jnp.concatenate([norm_back(d_norm, hat, inv)] * (chunk // cols), axis=0)

    def before(g, _):
        at = pl.ds(pl.multiple_of(g * chunk, chunk), chunk)
        grad = col_grad[at, :] + d_summary * weights[at, :]
        d_after[at, :] = grad
        rounded = grad.astype(BF16)
        dab_s[at, :] = rounded
        d_mixed = dot_nt(rounded, col_merge[...])
        for i in range(width // 128):
            dmix_s.at[i][at, :] = d_mixed[:, i * 128 : (i + 1) * 128]
        return 0

    lax.fori_loop(0, cells // chunk, before, 0)
    merge_g[...] = (dot_tn(col_mixed[...], dab_s[...]) * scale).astype(merge_g.dtype)
    allowed = column_allowed(rows, valid_keys[...])
    half = rows // 2
    per = width // 128

    def step(c, _):
        query, keys, values = column_parts([cqkv_s.at[i] for i in range(6)], [halo_s.at[i] for i in range(4)], c, rows, cols, width)
        here = pl.ds(c, rows, stride=cols)
        behind = pl.ds(c, half, stride=cols)
        grad = jnp.concatenate([dmix_s.at[i][here, :].astype(BF16) for i in range(per)], axis=1)
        dq, dk, dv = attend_back(query, keys, values, grad, allowed)
        for i in range(per):
            lanes = slice(i * 128, (i + 1) * 128)
            dqkv_s.at[i][here, :] = dq[:, lanes]
            dqkv_s.at[per + i][here, :] = dk[half:, lanes]
            dqkv_s.at[2 * per + i][here, :] = dv[half:, lanes]
            dhalo_s.at[i][behind, :] = dk[:half, lanes]
            dhalo_s.at[per + i][behind, :] = dv[:half, lanes]
        return 0

    lax.fori_loop(0, cols, step, 0)
    for i in range(3 * per):
        dqkv[:, i * 128 : (i + 1) * 128] = dqkv_s[i]
    for i in range(2 * per):
        halo_grad[:, i * 128 : (i + 1) * 128] = dhalo_s[i].astype(BF16)


def fifth_kernel(scale, dcol, edge_grad, d_after_in, after_rows, table, types, row_norm, row_qkv, row_mixed, col_norm, row_in, row_merge, col_in, table_grad, type_sum, row_in_g, row_merge_g, col_in_g, dcol_s, dab_s, drow_s):
    cells = types.shape[0]
    width = types.shape[1]
    groups = table.shape[0] // cells
    cols = type_sum.shape[0]
    allowed = row_allowed(cells, cols)
    type_sum[...] = jnp.zeros_like(type_sum)

    def step(g, _):
        at = pl.ds(pl.multiple_of(g * cells, cells), cells)
        late = (g >= groups // 2).astype(F32)
        edge_at = pl.ds(pl.multiple_of(jnp.maximum(g - groups // 2, 0) * cells, cells), cells)
        edge = edge_grad[edge_at, :].astype(F32) * late
        d_query = dcol[at, :width].astype(BF16)
        d_pairs = (dcol[at, width:] + edge).astype(BF16)
        d_qkv = jnp.concatenate([d_query, d_pairs], axis=1)
        dcol_s[at, :] = d_qkv
        hat, inv = norm(after_rows[at, :])
        d_after = d_after_in[at, :] + norm_back(dot_nt(d_qkv, col_in[...]), hat, inv)
        rounded = d_after.astype(BF16)
        dab_s[at, :] = rounded
        d_mixed = dot_nt(rounded, row_merge[...]).astype(BF16)
        qkv = row_qkv[at, :]
        dq, dk, dv = attend_back(qkv[:, :width], qkv[:, width : 2 * width], qkv[:, 2 * width :], d_mixed, allowed)
        d_row = jnp.concatenate([dq.astype(BF16), dk.astype(BF16), dv.astype(BF16)], axis=1)
        drow_s[at, :] = d_row
        hat, inv = norm(table[at, :].astype(F32) + types[...])
        d_res = d_after + norm_back(dot_nt(d_row, row_in[...]), hat, inv)
        table_grad[at, :] = d_res.astype(BF16)
        type_sum[...] += jnp.sum(d_res.reshape(cells // cols, cols, width), axis=0)
        return 0

    lax.fori_loop(0, groups, step, 0)
    col_in_g[...] = (dot_tn(col_norm[...], dcol_s[...]) * scale).astype(col_in_g.dtype)
    row_merge_g[...] = (dot_tn(row_mixed[...], dab_s[...]) * scale).astype(row_merge_g.dtype)
    row_in_g[...] = (dot_tn(row_norm[...], drow_s[...]) * scale).astype(row_in_g.dtype)


def call(body, outs, scratch, *args):
    return pl.pallas_call(
        body,
        out_shape=[jax.ShapeDtypeStruct(shape, kind) for shape, kind in outs],
        scratch_shapes=[pltpu.VMEM(shape, kind) for shape, kind in scratch],
        compiler_params=pltpu.CompilerParams(vmem_limit_bytes=VMEM_LIMIT),
    )(*args)


def shards(
    table, row_mask, column_types, type_table, row_inputs, row_merge, column_inputs, column_merge,
    summary_queries, summary_pairs, summary_merge, expand_weight, reduce_weight, out_cotangent,
):
    rows, cols, width = table.shape
    cells = rows * cols
    half = rows // 2
    hidden = expand_weight.shape[1]
    scale = 1.0 / math.sqrt(rows * lax.axis_size("rows") * cols)
    validity = row_mask.astype(F32)
    selector = (column_types[:, None] == jnp.arange(NTYPES, dtype=jnp.int32)[None, :]).astype(F32)
    types = jnp.dot(selector, type_table.astype(F32), precision=lax.Precision.HIGHEST)
    types = jnp.tile(types, (128 // cols, 1))
    first = (lax.axis_index("rows") > 0).astype(F32)
    valid_keys = jnp.concatenate([jnp.broadcast_to(first, (half,)), validity])[:, None]
    weights = jnp.repeat(validity / jnp.sum(validity), cols)[:, None]
    cell_table = table.reshape(cells, width)
    cot = out_cotangent.reshape(cells, width)

    row_norm, row_qkv, row_mixed, after_rows, col_norm, col_qkv, edge = call(
        first_kernel,
        [((cells, width), BF16), ((cells, 3 * width), BF16), ((cells, width), BF16), ((cells, width), F32),
         ((cells, width), BF16), ((cells, 3 * width), F32), ((half * cols, 2 * width), BF16)],
        [], cell_table, types, row_inputs, row_merge, column_inputs,
    )
    halo = from_behind(edge, "rows", 1)
    lanes = width // 128
    col_mixed, after_columns, summary, summary_norm, squery, skv = call(
        second_kernel,
        [((cells, width), BF16), ((cells, width), F32), ((cols, width), F32), ((cols, width), BF16),
         ((cols, width), BF16), ((cols, 2 * width), BF16)],
        [((3 * lanes, cells, 128), F32), ((2 * lanes, half * cols, 128), F32), ((lanes, cells, 128), F32)],
        after_rows, col_qkv, halo, valid_keys, weights, column_merge, summary_queries, summary_pairs,
    )
    every_pair = lax.all_gather(skv, "rows", axis=0, tiled=True)
    tokens = every_pair.shape[0]
    encoded, col_grad, query_grad, pair_grad, smerge_g, expand_g, reduce_g = call(
        partial(third_kernel, scale),
        [((cells, width), BF16), ((cells, width), F32), ((cols, width), BF16), ((tokens, 2 * width), F32),
         ((width, width), BF16), ((width, hidden), BF16), ((hidden, width), BF16)],
        [((cols, width), F32), ((cells, hidden), BF16), ((cells, width), BF16), ((cells, hidden), BF16)],
        after_columns, squery, every_pair, cot, summary_merge, expand_weight, reduce_weight,
    )
    pair_share = lax.psum_scatter(pair_grad, "rows", scatter_dimension=0, tiled=True)
    d_after, dqkv, halo_grad, queries_g, pairs_g, cmerge_g = call(
        partial(fourth_kernel, scale),
        [((cells, width), F32), ((cells, 3 * width), F32), ((half * cols, 2 * width), BF16),
         ((width, width), BF16), ((width, 2 * width), BF16), ((width, width), BF16)],
        [((3 * lanes, cells, 128), F32), ((2 * lanes, half * cols, 128), F32), ((lanes, cells, 128), F32),
         ((3 * lanes, cells, 128), F32), ((2 * lanes, half * cols, 128), F32), ((cells, width), BF16)],
        col_grad, query_grad, pair_share, summary, summary_norm, weights, col_qkv, halo, valid_keys, col_mixed,
        column_merge, summary_queries, summary_pairs,
    )
    edge_grad = from_behind(halo_grad, "rows", -1)
    table_grad, type_sum, row_in_g, row_merge_g, col_in_g = call(
        partial(fifth_kernel, scale),
        [((cells, width), BF16), ((cols, width), F32), ((width, 3 * width), BF16), ((width, width), BF16),
         ((width, 3 * width), BF16)],
        [((cells, 3 * width), BF16), ((cells, width), BF16), ((cells, 3 * width), BF16)],
        dqkv, edge_grad, d_after, after_rows, cell_table, types, row_norm, row_qkv, row_mixed, col_norm,
        row_inputs, row_merge, column_inputs,
    )
    type_g = (lax.dot_general(selector, type_sum, (((0,), (0,)), ((), ())), precision=lax.Precision.HIGHEST) * scale).astype(BF16)
    totals = lax.psum(
        (type_g, row_in_g, row_merge_g, col_in_g, cmerge_g, queries_g, pairs_g, smerge_g, expand_g, reduce_g), "rows"
    )
    return (encoded.reshape(table.shape), table_grad.reshape(table.shape)) + tuple(x.astype(F32) for x in totals)


def solution(mesh):
    split = P(("win", "rows"), None, None)
    return jax.shard_map(
        shards,
        mesh=mesh,
        in_specs=(split, P(("win", "rows")), P("win")) + (P(),) * 10 + (split,),
        out_specs=(split, split) + (P("win", None),) * 10,
        check_vma=False,
    )
```

```python
from functools import partial
import math

import jax
import jax.numpy as jnp
from jax import lax
from jax.experimental import pallas as pl
from jax.experimental.pallas import tpu as pltpu
from jax.sharding import PartitionSpec as P

HEADS = 8
NTYPES = 8
SPAN = 64
EPSILON = 1e-05
F32 = jnp.float32
BF16 = jnp.bfloat16
VMEM_LIMIT = 56 * 1024 * 1024


def from_behind(block, axis, distance):
    devices = range(lax.axis_size(axis))
    route = [(i - distance, i) for i in devices if i - distance in devices]
    return lax.ppermute(block, axis, route)


def dot_nn(a, b):
    return lax.dot_general(a, b, (((1,), (0,)), ((), ())), preferred_element_type=F32)


def dot_nt(a, b):
    return lax.dot_general(a, b, (((1,), (1,)), ((), ())), preferred_element_type=F32)


def dot_tn(a, b):
    return lax.dot_general(a, b, (((0,), (0,)), ((), ())), preferred_element_type=F32)


def norm(x):
    center = x - jnp.mean(x, axis=-1, keepdims=True)
    scale = lax.rsqrt(jnp.mean(center * center, axis=-1, keepdims=True) + EPSILON)
    return center * scale, scale


def norm_back(grad, hat, scale):
    first = jnp.mean(grad, axis=-1, keepdims=True)
    second = jnp.mean(grad * hat, axis=-1, keepdims=True)
    return scale * (grad - first - hat * second)


def stack_heads(x):
    head = lax.broadcasted_iota(jnp.int32, (1, x.shape[1]), 1) // (x.shape[1] // HEADS)
    return jnp.concatenate([x * (head == h).astype(F32).astype(BF16) for h in range(HEADS)], axis=0)


def merge_heads(x):
    n = x.shape[0] // HEADS
    head = lax.broadcasted_iota(jnp.int32, (n, x.shape[1]), 1) // (x.shape[1] // HEADS)
    out = x[:n]
    for h in range(1, HEADS):
        out = jnp.where(head == h, x[h * n : (h + 1) * n], out)
    return out


def shares_of(stacked, keys, allowed):
    width = keys.shape[1] // HEADS
    scores = jnp.exp2(dot_nt(keys, stacked) * (math.log2(math.e) / math.sqrt(width)))
    if allowed is not None:
        scores = jnp.where(allowed, scores, 0.0)
    total = jnp.sum(scores, axis=0, keepdims=True)
    return scores / total, total


def attend(query, keys, values, allowed):
    shares = shares_of(stack_heads(query), keys, allowed)[0].astype(BF16)
    return merge_heads(dot_tn(shares, values)).astype(BF16)


def attend_back(query, keys, values, grad, allowed):
    width = keys.shape[1] // HEADS
    stacked = stack_heads(query)
    grads = stack_heads(grad)
    shares = shares_of(stacked, keys, allowed)[0]
    share_grad = dot_nt(values, grads)
    total = jnp.sum(share_grad * shares, axis=0, keepdims=True)
    score_grad = (shares * (share_grad - total) * (1.0 / math.sqrt(width))).astype(BF16)
    query_grad = merge_heads(dot_tn(score_grad, keys))
    key_grad = dot_nn(score_grad, stacked)
    value_grad = dot_nn(shares.astype(BF16), grads)
    return query_grad, key_grad, value_grad


def query_back(query, keys, values, grad):
    width = keys.shape[1] // HEADS
    shares, norms = shares_of(stack_heads(query), keys, None)
    share_grad = dot_nt(values, stack_heads(grad))
    total = jnp.sum(share_grad * shares, axis=0, keepdims=True)
    score_grad = (shares * (share_grad - total) * (1.0 / math.sqrt(width))).astype(BF16)
    return merge_heads(dot_tn(score_grad, keys)), norms, total


def pair_back(queries, grads, lines, keys, values):
    width = keys.shape[1] // HEADS
    n = queries.shape[0]
    stacked = jnp.concatenate([stack_heads(queries[i]) for i in range(n)], axis=0)
    stacked_grads = jnp.concatenate([stack_heads(grads[i]) for i in range(n)], axis=0)
    norms = jnp.concatenate([lines[i][0:1] for i in range(n)], axis=1)
    total = jnp.concatenate([lines[i][1:2] for i in range(n)], axis=1)
    shares = jnp.exp2(dot_nt(keys, stacked) * (math.log2(math.e) / math.sqrt(width))) / norms
    share_grad = dot_nt(values, stacked_grads)
    score_grad = (shares * (share_grad - total) * (1.0 / math.sqrt(width))).astype(BF16)
    return dot_nn(score_grad, stacked), dot_nn(shares.astype(BF16), stacked_grads)


def row_allowed(cells, cols):
    key = lax.broadcasted_iota(jnp.int32, (cells, HEADS * cells), 0)
    query = lax.broadcasted_iota(jnp.int32, (cells, HEADS * cells), 1)
    return key // cols == (query % cells) // cols


def column_allowed(rows, valid):
    half = rows // 2
    shape = (rows + half, HEADS * rows)
    key = lax.broadcasted_iota(jnp.int32, shape, 0)
    start = (lax.broadcasted_iota(jnp.int32, shape, 1) % rows) // half * half
    return (key >= start) & (key < start + rows) & (valid > 0.5)


def first_kernel(table, types, row_in, row_merge, col_in, row_norm, row_qkv, row_mixed, after_rows, col_norm, col_qkv, edge):
    cells = types.shape[0]
    width = types.shape[1]
    groups = table.shape[0] // cells
    allowed = row_allowed(cells, 16)

    def step(g, _):
        at = pl.ds(pl.multiple_of(g * cells, cells), cells)
        residual = table[at, :].astype(F32) + types[...]
        normed = norm(residual)[0].astype(BF16)
        row_norm[at, :] = normed
        qkv = dot_nn(normed, row_in[...]).astype(BF16)
        row_qkv[at, :] = qkv
        mixed = attend(qkv[:, :width], qkv[:, width : 2 * width], qkv[:, 2 * width :], allowed)
        row_mixed[at, :] = mixed
        after = residual + dot_nn(mixed, row_merge[...])
        after_rows[at, :] = after
        cnormed = norm(after)[0].astype(BF16)
        col_norm[at, :] = cnormed
        cqkv = dot_nn(cnormed, col_in[...]).astype(BF16)
        col_qkv[at, :] = cqkv.astype(F32)

        @pl.when(g >= groups // 2)
        def _():
            edge[pl.ds(pl.multiple_of((g - groups // 2) * cells, cells), cells), :] = cqkv[:, width:]

        return 0

    lax.fori_loop(0, groups, step, 0)


def column_parts(cqkv, halo, column, rows, cols, width):
    here = pl.ds(column, rows, stride=cols)
    before = pl.ds(column, rows // 2, stride=cols)
    parts = []
    for i in range(width // 128 * 3):
        parts.append(cqkv[i][here, :].astype(BF16))
    halos = [halo[i][before, :].astype(BF16) for i in range(width // 128 * 2)]
    per = width // 128
    query = jnp.concatenate(parts[:per], axis=1)
    keys = jnp.concatenate([jnp.concatenate(halos[:per], axis=1), jnp.concatenate(parts[per : 2 * per], axis=1)], axis=0)
    values = jnp.concatenate([jnp.concatenate(halos[per:], axis=1), jnp.concatenate(parts[2 * per :], axis=1)], axis=0)
    return query, keys, values


def spread(src, dst):
    for i in range(dst.shape[0]):
        dst[i] = src[:, i * 128 : (i + 1) * 128].astype(F32)


def second_kernel(after_rows, cqkv, halo, valid_keys, weights, col_merge, squeries, spairs, col_mixed, after_columns, summary, summary_norm, squery, skv, cqkv_s, halo_s, mixed_s):
    cells, width = after_rows.shape
    rows = SPAN
    cols = cells // rows
    spread(cqkv, cqkv_s)
    spread(halo, halo_s)
    allowed = column_allowed(rows, valid_keys[...])

    def step(c, _):
        query, keys, values = column_parts([cqkv_s.at[i] for i in range(6)], [halo_s.at[i] for i in range(4)], c, rows, cols, width)
        mixed = attend(query, keys, values, allowed).astype(F32)
        for i in range(width // 128):
            mixed_s.at[i][pl.ds(c, rows, stride=cols), :] = mixed[:, i * 128 : (i + 1) * 128]
        return 0

    lax.fori_loop(0, cols, step, 0)
    chunk = 128
    summary[...] = jnp.zeros_like(summary)

    def merge(g, _):
        at = pl.ds(pl.multiple_of(g * chunk, chunk), chunk)
        mixed = jnp.concatenate([mixed_s.at[i][at, :] for i in range(width // 128)], axis=1).astype(BF16)
        col_mixed[at, :] = mixed
        after = after_rows[at, :] + dot_nn(mixed, col_merge[...])
        after_columns[at, :] = after
        weighted = after * weights[at, :]
        summary[...] += jnp.sum(weighted.reshape(chunk // cols, cols, width), axis=0)
        return 0

    lax.fori_loop(0, cells // chunk, merge, 0)
    normed = norm(summary[...])[0].astype(BF16)
    summary_norm[...] = normed
    squery[...] = dot_nn(normed, squeries[...]).astype(BF16)
    skv[...] = dot_nn(normed, spairs[...]).astype(BF16)


def gelu_parts(x):
    k = math.sqrt(2.0 / math.pi)
    t = jnp.tanh(k * (x + 0.044715 * x * x * x))
    value = 0.5 * x * (1.0 + t)
    slope = 0.5 * (1.0 + t) + 0.5 * x * (1.0 - t * t) * (k * (1.0 + 3 * 0.044715 * x * x))
    return value, slope


def third_kernel(scale, after_columns, squery, pairs, cot, smerge, expand, reduce, encoded, col_grad, query_grad, query_and_grad, lines, packed, span_s, hidden_s, feed_s, du_s):
    cells, width = after_columns.shape
    cols = squery.shape[0]
    query = squery[...]
    tokens = pairs.shape[0] * cols
    keys = pairs[:, :, :width].reshape(tokens, width)
    values = pairs[:, :, width:].reshape(tokens, width)
    mixed = attend(query, keys, values, None)
    chunk = 128
    term = jnp.concatenate([dot_nn(mixed, smerge[...])] * (chunk // cols), axis=0)
    span_s[...] = jnp.zeros_like(span_s)

    def step(g, _):
        at = pl.ds(pl.multiple_of(g * chunk, chunk), chunk)
        mixed_in = after_columns[at, :] + term
        hat, inv = norm(mixed_in)
        feed = hat.astype(BF16)
        value, slope = gelu_parts(dot_nn(feed, expand[...]))
        hidden = value.astype(BF16)
        encoded[at, :] = (mixed_in + dot_nn(hidden, reduce[...])).astype(BF16)
        g_out = cot[at, :]
        d_up = (dot_nt(g_out, reduce[...]) * slope).astype(BF16)
        d_feed = dot_nt(d_up, expand[...])
        d_in = g_out.astype(F32) + norm_back(d_feed, hat, inv)
        col_grad[at, :] = d_in
        span_s[...] += jnp.sum(d_in.reshape(chunk // cols, cols, width), axis=0)
        hidden_s[at, :] = hidden
        feed_s[at, :] = feed
        du_s[at, :] = d_up
        return 0

    lax.fori_loop(0, cells // chunk, step, 0)
    d_span = span_s[...].astype(BF16)
    packed[0] = (dot_tn(mixed, d_span) * scale).astype(BF16)
    d_mixed = dot_nt(d_span, smerge[...]).astype(BF16)
    dq, norms, total = query_back(query, keys, values, d_mixed)
    query_grad[...] = dq.astype(BF16)
    query_and_grad[:, :width] = query
    query_and_grad[:, width:] = d_mixed
    lines[...] = jnp.concatenate([norms, total, jnp.zeros((6, norms.shape[1]), F32)], axis=0)
    expand_g = (dot_tn(feed_s[...], du_s[...]) * scale).astype(BF16)
    reduce_g = (dot_tn(hidden_s[...], cot[...]) * scale).astype(BF16)
    for i in range(2):
        packed[1 + i] = expand_g[:, i * width : (i + 1) * width]
        packed[3 + i] = reduce_g[i * width : (i + 1) * width, :]


def fourth_kernel(scale, col_grad, query_grad, every_query, every_line, skv, summary, summary_norm, weights, cqkv, halo, valid_keys, col_mixed, col_merge, squeries, spairs, d_after, dqkv, halo_grad, packed, cqkv_s, halo_s, dmix_s, dqkv_s, dhalo_s, dab_s):
    cells, width = col_grad.shape
    rows = SPAN
    cols = cells // rows
    spread(cqkv, cqkv_s)
    spread(halo, halo_s)
    qg = query_grad[...]
    dk, dv = pair_back(every_query[:, :, :width], every_query[:, :, width:], every_line[...], skv[:, :width], skv[:, width:])
    pg = jnp.concatenate([dk.astype(BF16), dv.astype(BF16)], axis=1)
    packed[1] = (dot_tn(summary_norm[...], qg) * scale).astype(BF16)
    pairs_g = (dot_tn(summary_norm[...], pg) * scale).astype(BF16)
    for i in range(2):
        packed[2 + i] = pairs_g[:, i * width : (i + 1) * width]
    d_norm = dot_nt(qg, squeries[...]) + dot_nt(pg, spairs[...])
    hat, inv = norm(summary[...])
    chunk = 128
    d_summary = jnp.concatenate([norm_back(d_norm, hat, inv)] * (chunk // cols), axis=0)

    def before(g, _):
        at = pl.ds(pl.multiple_of(g * chunk, chunk), chunk)
        grad = col_grad[at, :] + d_summary * weights[at, :]
        d_after[at, :] = grad
        rounded = grad.astype(BF16)
        dab_s[at, :] = rounded
        d_mixed = dot_nt(rounded, col_merge[...])
        for i in range(width // 128):
            dmix_s.at[i][at, :] = d_mixed[:, i * 128 : (i + 1) * 128]
        return 0

    lax.fori_loop(0, cells // chunk, before, 0)
    packed[0] = (dot_tn(col_mixed[...], dab_s[...]) * scale).astype(BF16)
    allowed = column_allowed(rows, valid_keys[...])
    half = rows // 2
    per = width // 128

    def step(c, _):
        query, keys, values = column_parts([cqkv_s.at[i] for i in range(6)], [halo_s.at[i] for i in range(4)], c, rows, cols, width)
        here = pl.ds(c, rows, stride=cols)
        behind = pl.ds(c, half, stride=cols)
        grad = jnp.concatenate([dmix_s.at[i][here, :].astype(BF16) for i in range(per)], axis=1)
        dq, dk, dv = attend_back(query, keys, values, grad, allowed)
        for i in range(per):
            lanes = slice(i * 128, (i + 1) * 128)
            dqkv_s.at[i][here, :] = dq[:, lanes]
            dqkv_s.at[per + i][here, :] = dk[half:, lanes]
            dqkv_s.at[2 * per + i][here, :] = dv[half:, lanes]
            dhalo_s.at[i][behind, :] = dk[:half, lanes]
            dhalo_s.at[per + i][behind, :] = dv[:half, lanes]
        return 0

    lax.fori_loop(0, cols, step, 0)
    for i in range(3 * per):
        dqkv[:, i * 128 : (i + 1) * 128] = dqkv_s[i]
    for i in range(2 * per):
        halo_grad[:, i * 128 : (i + 1) * 128] = dhalo_s[i].astype(BF16)


def fifth_kernel(scale, dcol, edge_grad, d_after_in, after_rows, table, types, row_norm, row_qkv, row_mixed, col_norm, row_in, row_merge, col_in, table_grad, type_sum, packed, dcol_s, dab_s, drow_s):
    cells = types.shape[0]
    width = types.shape[1]
    groups = table.shape[0] // cells
    cols = type_sum.shape[0]
    allowed = row_allowed(cells, cols)
    type_sum[...] = jnp.zeros_like(type_sum)

    def step(g, _):
        at = pl.ds(pl.multiple_of(g * cells, cells), cells)
        late = (g >= groups // 2).astype(F32)
        edge_at = pl.ds(pl.multiple_of(jnp.maximum(g - groups // 2, 0) * cells, cells), cells)
        edge = edge_grad[edge_at, :].astype(F32) * late
        d_query = dcol[at, :width].astype(BF16)
        d_pairs = (dcol[at, width:] + edge).astype(BF16)
        d_qkv = jnp.concatenate([d_query, d_pairs], axis=1)
        dcol_s[at, :] = d_qkv
        hat, inv = norm(after_rows[at, :])
        d_after = d_after_in[at, :] + norm_back(dot_nt(d_qkv, col_in[...]), hat, inv)
        rounded = d_after.astype(BF16)
        dab_s[at, :] = rounded
        d_mixed = dot_nt(rounded, row_merge[...]).astype(BF16)
        qkv = row_qkv[at, :]
        dq, dk, dv = attend_back(qkv[:, :width], qkv[:, width : 2 * width], qkv[:, 2 * width :], d_mixed, allowed)
        d_row = jnp.concatenate([dq.astype(BF16), dk.astype(BF16), dv.astype(BF16)], axis=1)
        drow_s[at, :] = d_row
        hat, inv = norm(table[at, :].astype(F32) + types[...])
        d_res = d_after + norm_back(dot_nt(d_row, row_in[...]), hat, inv)
        table_grad[at, :] = d_res.astype(BF16)
        type_sum[...] += jnp.sum(d_res.reshape(cells // cols, cols, width), axis=0)
        return 0

    lax.fori_loop(0, groups, step, 0)
    col_in_g = (dot_tn(col_norm[...], dcol_s[...]) * scale).astype(BF16)
    row_in_g = (dot_tn(row_norm[...], drow_s[...]) * scale).astype(BF16)
    for i in range(3):
        packed[i] = row_in_g[:, i * width : (i + 1) * width]
        packed[3 + i] = col_in_g[:, i * width : (i + 1) * width]
    packed[6] = (dot_tn(row_mixed[...], dab_s[...]) * scale).astype(BF16)
    type_sum[...] = type_sum[...] * scale


def greet(peers):
    barrier = pltpu.get_barrier_semaphore()
    for peer in peers:
        pl.semaphore_signal(barrier, inc=1, device_id={"rows": peer}, device_id_type=pl.DeviceIdType.MESH)
    pl.semaphore_wait(barrier, len(peers))


def push(src, dst, send, recv, peer):
    copy = pltpu.make_async_remote_copy(
        src_ref=src, dst_ref=dst, send_sem=send, recv_sem=recv,
        device_id={"rows": peer}, device_id_type=pl.DeviceIdType.MESH,
    )
    copy.start()
    return copy


def gather_kernel(n, count, *refs):
    blocks, outs, holds, (send, recv) = refs[:count], refs[count : 2 * count], refs[2 * count : 3 * count], refs[3 * count :]
    me = lax.axis_index("rows")
    peers = [lax.rem(me + d, n) for d in range(1, n)]
    greet(peers)
    copies = []
    for d in range(n - 1):
        for i in range(count):
            copies.append(push(blocks[i], holds[i].at[me], send.at[i, d], recv.at[i, d], peers[d]))
    for i in range(count):
        holds[i][pl.ds(me, 1)] = blocks[i][...][None]
    for copy in copies:
        copy.wait()
    for i in range(count):
        outs[i][...] = holds[i][...]


def gather(n, identity, *blocks):
    vmem = pl.BlockSpec(memory_space=pltpu.VMEM)
    count = len(blocks)
    return pl.pallas_call(
        partial(gather_kernel, n, count),
        out_shape=[jax.ShapeDtypeStruct((n,) + x.shape, x.dtype) for x in blocks],
        in_specs=[vmem] * count,
        out_specs=[vmem] * count,
        scratch_shapes=[pltpu.VMEM((n,) + x.shape, x.dtype) for x in blocks]
        + [pltpu.SemaphoreType.DMA((count, n - 1)), pltpu.SemaphoreType.DMA((count, n - 1))],
        compiler_params=pltpu.CompilerParams(collective_id=identity, has_side_effects=True),
    )(*blocks)


def reduce_kernel(g3, g4, g5, sums, out, held, from_core, from_x, from_z, whole, send, recv):
    me = lax.axis_index("rows")
    core = lax.rem(me, 2)
    x = lax.rem(me // 2, 2)
    z = me // 4
    by_core = me + 1 - 2 * core
    by_x = me + 2 - 4 * x
    zs = [lax.rem(z + d, 4) for d in range(1, 4)]
    by_z = [other * 4 + x * 2 + core for other in zs]
    greet([by_core, by_x] + by_z)
    rows = g3.shape[1]
    index = 0
    for part in (g3, g4, g5):
        for i in range(part.shape[0]):
            held[index, :rows, :] = part[i]
            index += 1
    for i in range(16):
        held[i, rows:, :] = jnp.broadcast_to(sums[i : i + 1, :], (16, sums.shape[1])).astype(BF16)

    push(held.at[pl.ds((1 - core) * 8, 8)], from_core, send.at[0], recv.at[0], by_core).wait()

    def add_core(i, _):
        held[core * 8 + i] = (held[core * 8 + i].astype(F32) + from_core[i].astype(F32)).astype(BF16)
        return 0

    lax.fori_loop(0, 8, add_core, 0)
    push(held.at[pl.ds(core * 8 + (1 - x) * 4, 4)], from_x, send.at[1], recv.at[1], by_x).wait()
    base = core * 8 + x * 4

    def add_x(i, _):
        held[base + i] = (held[base + i].astype(F32) + from_x[i].astype(F32)).astype(BF16)
        return 0

    lax.fori_loop(0, 4, add_x, 0)
    copies = [push(held.at[base + zs[d]], from_z.at[d], send.at[2 + d], recv.at[2 + d], by_z[d]) for d in range(3)]
    for copy in copies:
        copy.wait()
    total = held[base + z].astype(F32)
    for d in range(3):
        total = total + from_z[d].astype(F32)
    mine = base + z
    whole[mine] = total.astype(BF16)
    copies = [push(whole.at[mine], whole.at[mine], send.at[5 + d], recv.at[5 + d], by_z[d]) for d in range(3)]
    for copy in copies:
        copy.wait()
    push(whole.at[pl.ds(base, 4)], whole.at[pl.ds(base, 4)], send.at[8], recv.at[8], by_x).wait()
    push(whole.at[pl.ds(core * 8, 8)], whole.at[pl.ds(core * 8, 8)], send.at[9], recv.at[9], by_core).wait()
    out[...] = whole[...]


def reduce_all(g3, g4, g5, sums):
    tall, width = g3.shape[1] + 16, g3.shape[2]
    vmem = pl.BlockSpec(memory_space=pltpu.VMEM)
    return pl.pallas_call(
        reduce_kernel,
        out_shape=jax.ShapeDtypeStruct((16, tall, width), BF16),
        in_specs=[vmem] * 4,
        out_specs=vmem,
        scratch_shapes=[pltpu.VMEM((count, tall, width), BF16) for count in (16, 8, 4, 3, 16)]
        + [pltpu.SemaphoreType.DMA((10,)), pltpu.SemaphoreType.DMA((10,))],
        compiler_params=pltpu.CompilerParams(collective_id=2, has_side_effects=True, vmem_limit_bytes=VMEM_LIMIT),
    )(g3, g4, g5, sums)


def unpack_kernel(packed, select, type_g, row_in_g, row_merge_g, col_in_g, cmerge_g, queries_g, pairs_g, smerge_g, expand_g, reduce_g):
    rows, width = cmerge_g.shape
    sums = jnp.concatenate([packed[i, rows:, :].astype(F32)[:1] for i in range(16)], axis=0).astype(BF16)
    type_g[...] = dot_tn(select[...], sums)

    def wide(out, start, count):
        for i in range(count):
            out[:, i * width : (i + 1) * width] = packed[start + i, :rows, :].astype(F32)

    wide(smerge_g, 0, 1)
    wide(expand_g, 1, 2)
    for i in range(2):
        reduce_g[i * rows : (i + 1) * rows, :] = packed[3 + i, :rows, :].astype(F32)
    wide(cmerge_g, 5, 1)
    wide(queries_g, 6, 1)
    wide(pairs_g, 7, 2)
    wide(row_in_g, 9, 3)
    wide(col_in_g, 12, 3)
    wide(row_merge_g, 15, 1)


def call(body, outs, scratch, *args):
    return pl.pallas_call(
        body,
        out_shape=[jax.ShapeDtypeStruct(shape, kind) for shape, kind in outs],
        scratch_shapes=[pltpu.VMEM(shape, kind) for shape, kind in scratch],
        compiler_params=pltpu.CompilerParams(vmem_limit_bytes=VMEM_LIMIT),
    )(*args)


def shards(
    table, row_mask, column_types, type_table, row_inputs, row_merge, column_inputs, column_merge,
    summary_queries, summary_pairs, summary_merge, expand_weight, reduce_weight, out_cotangent,
):
    rows, cols, width = table.shape
    cells = rows * cols
    half = rows // 2
    hidden = expand_weight.shape[1]
    scale = 1.0 / math.sqrt(rows * lax.axis_size("rows") * cols)
    validity = row_mask.astype(F32)
    selector = (column_types[:, None] == jnp.arange(NTYPES, dtype=jnp.int32)[None, :]).astype(F32)
    types = jnp.dot(selector, type_table.astype(F32), precision=lax.Precision.HIGHEST)
    types = jnp.tile(types, (128 // cols, 1))
    first = (lax.axis_index("rows") > 0).astype(F32)
    valid_keys = jnp.concatenate([jnp.broadcast_to(first, (half,)), validity])[:, None]
    weights = jnp.repeat(validity / jnp.sum(validity), cols)[:, None]
    cell_table = table.reshape(cells, width)
    cot = out_cotangent.reshape(cells, width)

    row_norm, row_qkv, row_mixed, after_rows, col_norm, col_qkv, edge = call(
        first_kernel,
        [((cells, width), BF16), ((cells, 3 * width), BF16), ((cells, width), BF16), ((cells, width), F32),
         ((cells, width), BF16), ((cells, 3 * width), F32), ((half * cols, 2 * width), BF16)],
        [], cell_table, types, row_inputs, row_merge, column_inputs,
    )
    halo = from_behind(edge, "rows", 1)
    lanes = width // 128
    col_mixed, after_columns, summary, summary_norm, squery, skv = call(
        second_kernel,
        [((cells, width), BF16), ((cells, width), F32), ((cols, width), F32), ((cols, width), BF16),
         ((cols, width), BF16), ((cols, 2 * width), BF16)],
        [((3 * lanes, cells, 128), F32), ((2 * lanes, half * cols, 128), F32), ((lanes, cells, 128), F32)],
        after_rows, col_qkv, halo, valid_keys, weights, column_merge, summary_queries, summary_pairs,
    )
    n = lax.axis_size("rows")
    (every_pair,) = gather(n, 0, skv)
    encoded, col_grad, query_grad, query_and_grad, lines, packed3 = call(
        partial(third_kernel, scale),
        [((cells, width), BF16), ((cells, width), F32), ((cols, width), BF16), ((cols, 2 * width), BF16),
         ((8, HEADS * cols), F32), ((5, width, width), BF16)],
        [((cols, width), F32), ((cells, hidden), BF16), ((cells, width), BF16), ((cells, hidden), BF16)],
        after_columns, squery, every_pair, cot, summary_merge, expand_weight, reduce_weight,
    )
    every_query, every_line = gather(n, 1, query_and_grad, lines)
    d_after, dqkv, halo_grad, packed4 = call(
        partial(fourth_kernel, scale),
        [((cells, width), F32), ((cells, 3 * width), F32), ((half * cols, 2 * width), BF16), ((4, width, width), BF16)],
        [((3 * lanes, cells, 128), F32), ((2 * lanes, half * cols, 128), F32), ((lanes, cells, 128), F32),
         ((3 * lanes, cells, 128), F32), ((2 * lanes, half * cols, 128), F32), ((cells, width), BF16)],
        col_grad, query_grad, every_query, every_line, skv, summary, summary_norm, weights, col_qkv, halo, valid_keys,
        col_mixed, column_merge, summary_queries, summary_pairs,
    )
    edge_grad = from_behind(halo_grad, "rows", -1)
    table_grad, type_sum, packed5 = call(
        partial(fifth_kernel, scale),
        [((cells, width), BF16), ((cols, width), F32), ((7, width, width), BF16)],
        [((cells, 3 * width), BF16), ((cells, width), BF16), ((cells, 3 * width), BF16)],
        dqkv, edge_grad, d_after, after_rows, cell_table, types, row_norm, row_qkv, row_mixed, col_norm,
        row_inputs, row_merge, column_inputs,
    )
    if n == 16:
        packed = reduce_all(packed3, packed4, packed5, type_sum)
    else:
        blocks = jnp.concatenate([packed3, packed4, packed5], axis=0)
        extra = jnp.broadcast_to(type_sum.astype(BF16)[:, None], (cols, 16, width))
        packed = lax.psum(jnp.concatenate([blocks, extra], axis=1), "rows")
    totals = call(
        unpack_kernel,
        [((NTYPES, width), F32), ((width, 3 * width), F32), ((width, width), F32), ((width, 3 * width), F32),
         ((width, width), F32), ((width, width), F32), ((width, 2 * width), F32), ((width, width), F32),
         ((width, hidden), F32), ((hidden, width), F32)],
        [], packed, selector.astype(BF16),
    )
    return (encoded.reshape(table.shape), table_grad.reshape(table.shape)) + tuple(totals)


def solution(mesh):
    split = P(("win", "rows"), None, None)
    return jax.shard_map(
        shards,
        mesh=mesh,
        in_specs=(split, P(("win", "rows")), P("win")) + (P(),) * 10 + (split,),
        out_specs=(split, split) + (P("win", None),) * 10,
        check_vma=False,
    )
```

```python
from functools import partial
import math

import jax
import jax.numpy as jnp
from jax import lax
from jax.experimental import pallas as pl
from jax.experimental.pallas import tpu as pltpu
from jax.sharding import PartitionSpec as P

HEADS = 8
NTYPES = 8
SPAN = 64
EPSILON = 1e-05
F32 = jnp.float32
BF16 = jnp.bfloat16
VMEM_LIMIT = 56 * 1024 * 1024


def from_behind(block, axis, distance):
    devices = range(lax.axis_size(axis))
    route = [(i - distance, i) for i in devices if i - distance in devices]
    return lax.ppermute(block, axis, route)


def dot_nn(a, b):
    return lax.dot_general(a, b, (((1,), (0,)), ((), ())), preferred_element_type=F32)


def dot_nt(a, b):
    return lax.dot_general(a, b, (((1,), (1,)), ((), ())), preferred_element_type=F32)


def dot_tn(a, b):
    return lax.dot_general(a, b, (((0,), (0,)), ((), ())), preferred_element_type=F32)


def norm(x):
    center = x - jnp.mean(x, axis=-1, keepdims=True)
    scale = lax.rsqrt(jnp.mean(center * center, axis=-1, keepdims=True) + EPSILON)
    return center * scale, scale


def norm_back(grad, hat, scale):
    first = jnp.mean(grad, axis=-1, keepdims=True)
    second = jnp.mean(grad * hat, axis=-1, keepdims=True)
    return scale * (grad - first - hat * second)


def stack_heads(x):
    head = lax.broadcasted_iota(jnp.int32, (1, x.shape[1]), 1) // (x.shape[1] // HEADS)
    return jnp.concatenate([x * (head == h).astype(F32).astype(BF16) for h in range(HEADS)], axis=0)


def merge_heads(x):
    n = x.shape[0] // HEADS
    head = lax.broadcasted_iota(jnp.int32, (n, x.shape[1]), 1) // (x.shape[1] // HEADS)
    out = x[:n]
    for h in range(1, HEADS):
        out = jnp.where(head == h, x[h * n : (h + 1) * n], out)
    return out


def shares_of(stacked, keys, allowed):
    width = keys.shape[1] // HEADS
    scores = jnp.exp2(dot_nt(keys, stacked) * (math.log2(math.e) / math.sqrt(width)))
    if allowed is not None:
        scores = jnp.where(allowed, scores, 0.0)
    total = jnp.sum(scores, axis=0, keepdims=True)
    return scores / total, total


def attend(query, keys, values, allowed):
    shares = shares_of(stack_heads(query), keys, allowed)[0].astype(BF16)
    return merge_heads(dot_tn(shares, values)).astype(BF16)


def attend_back(query, keys, values, grad, allowed):
    width = keys.shape[1] // HEADS
    stacked = stack_heads(query)
    grads = stack_heads(grad)
    shares = shares_of(stacked, keys, allowed)[0]
    share_grad = dot_nt(values, grads)
    total = jnp.sum(share_grad * shares, axis=0, keepdims=True)
    score_grad = (shares * (share_grad - total) * (1.0 / math.sqrt(width))).astype(BF16)
    query_grad = merge_heads(dot_tn(score_grad, keys))
    key_grad = dot_nn(score_grad, stacked)
    value_grad = dot_nn(shares.astype(BF16), grads)
    return query_grad, key_grad, value_grad


def query_back(query, keys, values, grad):
    width = keys.shape[1] // HEADS
    shares, norms = shares_of(stack_heads(query), keys, None)
    share_grad = dot_nt(values, stack_heads(grad))
    total = jnp.sum(share_grad * shares, axis=0, keepdims=True)
    score_grad = (shares * (share_grad - total) * (1.0 / math.sqrt(width))).astype(BF16)
    return merge_heads(dot_tn(score_grad, keys)), norms, total


def pair_back(queries, grads, lines, keys, values):
    width = keys.shape[1] // HEADS
    n = queries.shape[0]
    stacked = jnp.concatenate([stack_heads(queries[i]) for i in range(n)], axis=0)
    stacked_grads = jnp.concatenate([stack_heads(grads[i]) for i in range(n)], axis=0)
    norms = jnp.concatenate([lines[i][0:1] for i in range(n)], axis=1)
    total = jnp.concatenate([lines[i][1:2] for i in range(n)], axis=1)
    shares = jnp.exp2(dot_nt(keys, stacked) * (math.log2(math.e) / math.sqrt(width))) / norms
    share_grad = dot_nt(values, stacked_grads)
    score_grad = (shares * (share_grad - total) * (1.0 / math.sqrt(width))).astype(BF16)
    return dot_nn(score_grad, stacked), dot_nn(shares.astype(BF16), stacked_grads)


def row_allowed(cells, cols):
    key = lax.broadcasted_iota(jnp.int32, (cells, HEADS * cells), 0)
    query = lax.broadcasted_iota(jnp.int32, (cells, HEADS * cells), 1)
    return key // cols == (query % cells) // cols


def column_allowed(rows, valid):
    half = rows // 2
    shape = (rows + half, HEADS * rows)
    key = lax.broadcasted_iota(jnp.int32, shape, 0)
    start = (lax.broadcasted_iota(jnp.int32, shape, 1) % rows) // half * half
    spot = (key - half).astype(F32)
    present = (spot < valid[0:1, 0:1]) & (spot >= -half * valid[1:2, 0:1])
    return (key >= start) & (key < start + rows) & present


def cell_weights(start, count, cols, valid):
    row = (start + lax.broadcasted_iota(jnp.int32, (count, 1), 0)) // cols
    total = valid[0:1, 0:1]
    return jnp.where(row.astype(F32) < total, 1.0 / total, 0.0)


def first_kernel(table, types, row_in, row_merge, col_in, row_norm, row_qkv, row_mixed, after_rows, col_norm, col_qkv, edge):
    cells = types.shape[0]
    width = types.shape[1]
    groups = table.shape[0] // cells
    allowed = row_allowed(cells, 16)

    def step(g, _):
        at = pl.ds(pl.multiple_of(g * cells, cells), cells)
        residual = table[at, :].astype(F32) + types[...]
        normed = norm(residual)[0].astype(BF16)
        row_norm[at, :] = normed
        qkv = dot_nn(normed, row_in[...]).astype(BF16)
        row_qkv[at, :] = qkv
        mixed = attend(qkv[:, :width], qkv[:, width : 2 * width], qkv[:, 2 * width :], allowed)
        row_mixed[at, :] = mixed
        after = residual + dot_nn(mixed, row_merge[...])
        after_rows[at, :] = after
        cnormed = norm(after)[0].astype(BF16)
        col_norm[at, :] = cnormed
        cqkv = dot_nn(cnormed, col_in[...]).astype(BF16)
        col_qkv[at, :] = cqkv.astype(F32)

        @pl.when(g >= groups // 2)
        def _():
            edge[pl.ds(pl.multiple_of((g - groups // 2) * cells, cells), cells), :] = cqkv[:, width:]

        return 0

    lax.fori_loop(0, groups, step, 0, unroll=2)


def column_parts(cqkv, halo, column, rows, cols, width):
    here = pl.ds(column, rows, stride=cols)
    before = pl.ds(column, rows // 2, stride=cols)
    parts = []
    for i in range(width // 128 * 3):
        parts.append(cqkv[i][here, :].astype(BF16))
    halos = [halo[i][before, :].astype(BF16) for i in range(width // 128 * 2)]
    per = width // 128
    query = jnp.concatenate(parts[:per], axis=1)
    keys = jnp.concatenate([jnp.concatenate(halos[:per], axis=1), jnp.concatenate(parts[per : 2 * per], axis=1)], axis=0)
    values = jnp.concatenate([jnp.concatenate(halos[per:], axis=1), jnp.concatenate(parts[2 * per :], axis=1)], axis=0)
    return query, keys, values


def spread(src, dst):
    for i in range(dst.shape[0]):
        dst[i] = src[:, i * 128 : (i + 1) * 128].astype(F32)


def second_kernel(after_rows, cqkv, halo, valid, col_merge, squeries, spairs, col_mixed, after_columns, summary, summary_norm, squery, skv, cqkv_s, halo_s, mixed_s):
    cells, width = after_rows.shape
    rows = SPAN
    cols = cells // rows
    spread(cqkv, cqkv_s)
    spread(halo, halo_s)
    allowed = column_allowed(rows, valid)

    def step(c, _):
        query, keys, values = column_parts([cqkv_s.at[i] for i in range(6)], [halo_s.at[i] for i in range(4)], c, rows, cols, width)
        mixed = attend(query, keys, values, allowed).astype(F32)
        for i in range(width // 128):
            mixed_s.at[i][pl.ds(c, rows, stride=cols), :] = mixed[:, i * 128 : (i + 1) * 128]
        return 0

    lax.fori_loop(0, cols, step, 0, unroll=2)
    chunk = 128
    summary[...] = jnp.zeros_like(summary)

    def merge(g, _):
        at = pl.ds(pl.multiple_of(g * chunk, chunk), chunk)
        mixed = jnp.concatenate([mixed_s.at[i][at, :] for i in range(width // 128)], axis=1).astype(BF16)
        col_mixed[at, :] = mixed
        after = after_rows[at, :] + dot_nn(mixed, col_merge[...])
        after_columns[at, :] = after
        weighted = after * cell_weights(g * chunk, chunk, cols, valid)
        summary[...] += jnp.sum(weighted.reshape(chunk // cols, cols, width), axis=0)
        return 0

    lax.fori_loop(0, cells // chunk, merge, 0, unroll=2)
    normed = norm(summary[...])[0].astype(BF16)
    summary_norm[...] = normed
    squery[...] = dot_nn(normed, squeries[...]).astype(BF16)
    skv[...] = dot_nn(normed, spairs[...]).astype(BF16)


def gelu_parts(x):
    k = math.sqrt(2.0 / math.pi)
    t = jnp.tanh(k * (x + 0.044715 * x * x * x))
    value = 0.5 * x * (1.0 + t)
    slope = 0.5 * (1.0 + t) + 0.5 * x * (1.0 - t * t) * (k * (1.0 + 3 * 0.044715 * x * x))
    return value, slope


def third_kernel(scale, after_columns, squery, pairs, cot, smerge, expand, reduce, encoded, col_grad, query_grad, query_and_grad, lines, packed, span_s, hidden_s, feed_s, du_s):
    cells, width = after_columns.shape
    cols = squery.shape[0]
    query = squery[...]
    tokens = pairs.shape[0] * cols
    keys = pairs[:, :, :width].reshape(tokens, width)
    values = pairs[:, :, width:].reshape(tokens, width)
    mixed = attend(query, keys, values, None)
    chunk = 128
    term = jnp.concatenate([dot_nn(mixed, smerge[...])] * (chunk // cols), axis=0)
    span_s[...] = jnp.zeros_like(span_s)

    def step(g, _):
        at = pl.ds(pl.multiple_of(g * chunk, chunk), chunk)
        mixed_in = after_columns[at, :] + term
        hat, inv = norm(mixed_in)
        feed = hat.astype(BF16)
        value, slope = gelu_parts(dot_nn(feed, expand[...]))
        hidden = value.astype(BF16)
        encoded[at, :] = (mixed_in + dot_nn(hidden, reduce[...])).astype(BF16)
        g_out = cot[at, :]
        d_up = (dot_nt(g_out, reduce[...]) * slope).astype(BF16)
        d_feed = dot_nt(d_up, expand[...])
        d_in = g_out.astype(F32) + norm_back(d_feed, hat, inv)
        col_grad[at, :] = d_in
        span_s[...] += jnp.sum(d_in.reshape(chunk // cols, cols, width), axis=0)
        hidden_s[at, :] = hidden
        feed_s[at, :] = feed
        du_s[at, :] = d_up
        return 0

    lax.fori_loop(0, cells // chunk, step, 0, unroll=2)
    d_span = span_s[...].astype(BF16)
    packed[0] = (dot_tn(mixed, d_span) * scale).astype(BF16)
    d_mixed = dot_nt(d_span, smerge[...]).astype(BF16)
    dq, norms, total = query_back(query, keys, values, d_mixed)
    query_grad[...] = dq.astype(BF16)
    query_and_grad[:, :width] = query
    query_and_grad[:, width:] = d_mixed
    lines[...] = jnp.concatenate([norms, total, jnp.zeros((6, norms.shape[1]), F32)], axis=0)
    expand_g = (dot_tn(feed_s[...], du_s[...]) * scale).astype(BF16)
    reduce_g = (dot_tn(hidden_s[...], cot[...]) * scale).astype(BF16)
    for i in range(2):
        packed[1 + i] = expand_g[:, i * width : (i + 1) * width]
        packed[3 + i] = reduce_g[i * width : (i + 1) * width, :]


def fourth_kernel(scale, col_grad, query_grad, every_query, every_line, skv, summary, summary_norm, cqkv, halo, valid, col_mixed, col_merge, squeries, spairs, d_after, dqkv, halo_grad, packed, cqkv_s, halo_s, dmix_s, dqkv_s, dhalo_s, dab_s):
    cells, width = col_grad.shape
    rows = SPAN
    cols = cells // rows
    spread(cqkv, cqkv_s)
    spread(halo, halo_s)
    qg = query_grad[...]
    dk, dv = pair_back(every_query[:, :, :width], every_query[:, :, width:], every_line[...], skv[:, :width], skv[:, width:])
    pg = jnp.concatenate([dk.astype(BF16), dv.astype(BF16)], axis=1)
    packed[1] = (dot_tn(summary_norm[...], qg) * scale).astype(BF16)
    pairs_g = (dot_tn(summary_norm[...], pg) * scale).astype(BF16)
    for i in range(2):
        packed[2 + i] = pairs_g[:, i * width : (i + 1) * width]
    d_norm = dot_nt(qg, squeries[...]) + dot_nt(pg, spairs[...])
    hat, inv = norm(summary[...])
    chunk = 128
    d_summary = jnp.concatenate([norm_back(d_norm, hat, inv)] * (chunk // cols), axis=0)

    def before(g, _):
        at = pl.ds(pl.multiple_of(g * chunk, chunk), chunk)
        grad = col_grad[at, :] + d_summary * cell_weights(g * chunk, chunk, cols, valid)
        d_after[at, :] = grad
        rounded = grad.astype(BF16)
        dab_s[at, :] = rounded
        d_mixed = dot_nt(rounded, col_merge[...])
        for i in range(width // 128):
            dmix_s.at[i][at, :] = d_mixed[:, i * 128 : (i + 1) * 128]
        return 0

    lax.fori_loop(0, cells // chunk, before, 0, unroll=2)
    packed[0] = (dot_tn(col_mixed[...], dab_s[...]) * scale).astype(BF16)
    allowed = column_allowed(rows, valid)
    half = rows // 2
    per = width // 128

    def step(c, _):
        query, keys, values = column_parts([cqkv_s.at[i] for i in range(6)], [halo_s.at[i] for i in range(4)], c, rows, cols, width)
        here = pl.ds(c, rows, stride=cols)
        behind = pl.ds(c, half, stride=cols)
        grad = jnp.concatenate([dmix_s.at[i][here, :].astype(BF16) for i in range(per)], axis=1)
        dq, dk, dv = attend_back(query, keys, values, grad, allowed)
        for i in range(per):
            lanes = slice(i * 128, (i + 1) * 128)
            dqkv_s.at[i][here, :] = dq[:, lanes]
            dqkv_s.at[per + i][here, :] = dk[half:, lanes]
            dqkv_s.at[2 * per + i][here, :] = dv[half:, lanes]
            dhalo_s.at[i][behind, :] = dk[:half, lanes]
            dhalo_s.at[per + i][behind, :] = dv[:half, lanes]
        return 0

    lax.fori_loop(0, cols, step, 0, unroll=2)
    for i in range(3 * per):
        dqkv[:, i * 128 : (i + 1) * 128] = dqkv_s[i]
    for i in range(2 * per):
        halo_grad[:, i * 128 : (i + 1) * 128] = dhalo_s[i].astype(BF16)


def fifth_kernel(scale, dcol, edge_grad, d_after_in, after_rows, table, types, row_norm, row_qkv, row_mixed, col_norm, row_in, row_merge, col_in, table_grad, type_sum, packed, dcol_s, dab_s, drow_s):
    cells = types.shape[0]
    width = types.shape[1]
    groups = table.shape[0] // cells
    cols = type_sum.shape[0]
    allowed = row_allowed(cells, cols)
    type_sum[...] = jnp.zeros_like(type_sum)

    def step(g, _):
        at = pl.ds(pl.multiple_of(g * cells, cells), cells)
        late = (g >= groups // 2).astype(F32)
        edge_at = pl.ds(pl.multiple_of(jnp.maximum(g - groups // 2, 0) * cells, cells), cells)
        edge = edge_grad[edge_at, :].astype(F32) * late
        d_query = dcol[at, :width].astype(BF16)
        d_pairs = (dcol[at, width:] + edge).astype(BF16)
        d_qkv = jnp.concatenate([d_query, d_pairs], axis=1)
        dcol_s[at, :] = d_qkv
        hat, inv = norm(after_rows[at, :])
        d_after = d_after_in[at, :] + norm_back(dot_nt(d_qkv, col_in[...]), hat, inv)
        rounded = d_after.astype(BF16)
        dab_s[at, :] = rounded
        d_mixed = dot_nt(rounded, row_merge[...]).astype(BF16)
        qkv = row_qkv[at, :]
        dq, dk, dv = attend_back(qkv[:, :width], qkv[:, width : 2 * width], qkv[:, 2 * width :], d_mixed, allowed)
        d_row = jnp.concatenate([dq.astype(BF16), dk.astype(BF16), dv.astype(BF16)], axis=1)
        drow_s[at, :] = d_row
        hat, inv = norm(table[at, :].astype(F32) + types[...])
        d_res = d_after + norm_back(dot_nt(d_row, row_in[...]), hat, inv)
        table_grad[at, :] = d_res.astype(BF16)
        type_sum[...] += jnp.sum(d_res.reshape(cells // cols, cols, width), axis=0)
        return 0

    lax.fori_loop(0, groups, step, 0, unroll=2)
    col_in_g = (dot_tn(col_norm[...], dcol_s[...]) * scale).astype(BF16)
    row_in_g = (dot_tn(row_norm[...], drow_s[...]) * scale).astype(BF16)
    for i in range(3):
        packed[i] = row_in_g[:, i * width : (i + 1) * width]
        packed[3 + i] = col_in_g[:, i * width : (i + 1) * width]
    packed[6] = (dot_tn(row_mixed[...], dab_s[...]) * scale).astype(BF16)
    type_sum[...] = type_sum[...] * scale


def greet(peers):
    barrier = pltpu.get_barrier_semaphore()
    for peer in peers:
        pl.semaphore_signal(barrier, inc=1, device_id={"rows": peer}, device_id_type=pl.DeviceIdType.MESH)
    pl.semaphore_wait(barrier, len(peers))


def push(src, dst, send, recv, peer):
    copy = pltpu.make_async_remote_copy(
        src_ref=src, dst_ref=dst, send_sem=send, recv_sem=recv,
        device_id={"rows": peer}, device_id_type=pl.DeviceIdType.MESH,
    )
    copy.start()
    return copy


def gather_kernel(n, count, *refs):
    blocks, outs, holds, (send, recv) = refs[:count], refs[count : 2 * count], refs[2 * count : 3 * count], refs[3 * count :]
    me = lax.axis_index("rows")
    peers = [lax.rem(me + d, n) for d in range(1, n)]
    greet(peers)
    copies = []
    for d in range(n - 1):
        for i in range(count):
            copies.append(push(blocks[i], holds[i].at[me], send.at[i, d], recv.at[i, d], peers[d]))
    for i in range(count):
        holds[i][pl.ds(me, 1)] = blocks[i][...][None]
    for copy in copies:
        copy.wait()
    for i in range(count):
        outs[i][...] = holds[i][...]


def gather(n, identity, *blocks):
    vmem = pl.BlockSpec(memory_space=pltpu.VMEM)
    count = len(blocks)
    return pl.pallas_call(
        partial(gather_kernel, n, count),
        out_shape=[jax.ShapeDtypeStruct((n,) + x.shape, x.dtype) for x in blocks],
        in_specs=[vmem] * count,
        out_specs=[vmem] * count,
        scratch_shapes=[pltpu.VMEM((n,) + x.shape, x.dtype) for x in blocks]
        + [pltpu.SemaphoreType.DMA((count, n - 1)), pltpu.SemaphoreType.DMA((count, n - 1))],
        compiler_params=pltpu.CompilerParams(collective_id=identity, has_side_effects=True),
    )(*blocks)


def reduce_kernel(g3, g4, g5, sums, out, held, from_core, from_x, from_z, whole, send, recv):
    me = lax.axis_index("rows")
    core = lax.rem(me, 2)
    x = lax.rem(me // 2, 2)
    z = me // 4
    by_core = me + 1 - 2 * core
    by_x = me + 2 - 4 * x
    zs = [lax.rem(z + d, 4) for d in range(1, 4)]
    by_z = [other * 4 + x * 2 + core for other in zs]
    greet([by_core, by_x] + by_z)
    rows = g3.shape[1]
    index = 0
    for part in (g3, g4, g5):
        for i in range(part.shape[0]):
            held[index, :rows, :] = part[i]
            index += 1
    for i in range(16):
        held[i, rows:, :] = jnp.broadcast_to(sums[i : i + 1, :], (16, sums.shape[1])).astype(BF16)

    base = core * 8 + x * 4
    mine = base + z
    tall = rows + 16
    cuts = [0, tall - 3 * (rows // 4)] + [tall - k * (rows // 4) for k in (2, 1, 0)]
    chunks = [slice(cuts[c], cuts[c + 1]) for c in range(4)]
    sizes = [cuts[c + 1] - cuts[c] for c in range(4)]
    flying = {}

    def part(ref, c, at):
        return ref.at[at, pl.ds(cuts[c], sizes[c])]

    def finish(c):
        for copy in flying.pop(c):
            copy.wait()

    def core_out(c):
        at = pl.ds((1 - core) * 8, 8)
        flying[c] = [push(part(held, c, at), part(from_core, c, pl.ds(0, 8)), send.at[0, c], recv.at[0, c], by_core)]

    def x_out(c):
        finish(c)
        for i in range(8):
            total = held[core * 8 + i, chunks[c], :].astype(F32) + from_core[i, chunks[c], :].astype(F32)
            held[core * 8 + i, chunks[c], :] = total.astype(BF16)
        at = pl.ds(core * 8 + (1 - x) * 4, 4)
        flying[c] = [push(part(held, c, at), part(from_x, c, pl.ds(0, 4)), send.at[1, c], recv.at[1, c], by_x)]

    def z_out(c):
        finish(c)
        for i in range(4):
            total = held[base + i, chunks[c], :].astype(F32) + from_x[i, chunks[c], :].astype(F32)
            held[base + i, chunks[c], :] = total.astype(BF16)
        flying[c] = [
            push(part(held, c, base + zs[d]), part(from_z, c, d), send.at[2 + d, c], recv.at[2 + d, c], by_z[d])
            for d in range(3)
        ]

    def z_back(c):
        finish(c)
        total = held[mine, chunks[c], :].astype(F32)
        for d in range(3):
            total = total + from_z[d, chunks[c], :].astype(F32)
        whole[mine, chunks[c], :] = total.astype(BF16)
        flying[c] = [
            push(part(whole, c, mine), part(whole, c, mine), send.at[5 + d, c], recv.at[5 + d, c], by_z[d]) for d in range(3)
        ]

    def x_back(c):
        finish(c)
        at = pl.ds(base, 4)
        flying[c] = [push(part(whole, c, at), part(whole, c, at), send.at[8, c], recv.at[8, c], by_x)]

    def core_back(c):
        finish(c)
        at = pl.ds(core * 8, 8)
        flying[c] = [push(part(whole, c, at), part(whole, c, at), send.at[9, c], recv.at[9, c], by_core)]

    stages = [core_out, x_out, z_out, z_back, x_back, core_back, finish]
    for tick in range(4 + len(stages) - 1):
        for number in reversed(range(len(stages))):
            if 0 <= tick - number < 4:
                stages[number](tick - number)
    out[...] = whole[...]


def reduce_all(g3, g4, g5, sums):
    tall, width = g3.shape[1] + 16, g3.shape[2]
    vmem = pl.BlockSpec(memory_space=pltpu.VMEM)
    return pl.pallas_call(
        reduce_kernel,
        out_shape=jax.ShapeDtypeStruct((16, tall, width), BF16),
        in_specs=[vmem] * 4,
        out_specs=vmem,
        scratch_shapes=[pltpu.VMEM((count, tall, width), BF16) for count in (16, 8, 4, 3, 16)]
        + [pltpu.SemaphoreType.DMA((10, 4)), pltpu.SemaphoreType.DMA((10, 4))],
        compiler_params=pltpu.CompilerParams(collective_id=2, has_side_effects=True, vmem_limit_bytes=VMEM_LIMIT),
    )(g3, g4, g5, sums)


def unpack_kernel(packed, select, type_g, row_in_g, row_merge_g, col_in_g, cmerge_g, queries_g, pairs_g, smerge_g, expand_g, reduce_g):
    rows, width = cmerge_g.shape
    sums = jnp.concatenate([packed[i, rows:, :].astype(F32)[:1] for i in range(16)], axis=0).astype(BF16)
    type_g[...] = dot_tn(select[...], sums)

    def wide(out, start, count):
        for i in range(count):
            out[:, i * width : (i + 1) * width] = packed[start + i, :rows, :].astype(F32)

    wide(smerge_g, 0, 1)
    wide(expand_g, 1, 2)
    for i in range(2):
        reduce_g[i * rows : (i + 1) * rows, :] = packed[3 + i, :rows, :].astype(F32)
    wide(cmerge_g, 5, 1)
    wide(queries_g, 6, 1)
    wide(pairs_g, 7, 2)
    wide(row_in_g, 9, 3)
    wide(col_in_g, 12, 3)
    wide(row_merge_g, 15, 1)


def call(body, outs, scratch, *args):
    return pl.pallas_call(
        body,
        out_shape=[jax.ShapeDtypeStruct(shape, kind) for shape, kind in outs],
        scratch_shapes=[pltpu.VMEM(shape, kind) for shape, kind in scratch],
        compiler_params=pltpu.CompilerParams(vmem_limit_bytes=VMEM_LIMIT),
    )(*args)


def shards(
    table, row_mask, column_types, type_table, row_inputs, row_merge, column_inputs, column_merge,
    summary_queries, summary_pairs, summary_merge, expand_weight, reduce_weight, out_cotangent,
):
    rows, cols, width = table.shape
    cells = rows * cols
    half = rows // 2
    hidden = expand_weight.shape[1]
    scale = 1.0 / math.sqrt(rows * lax.axis_size("rows") * cols)
    validity = row_mask.astype(F32)
    selector = (column_types[:, None] == jnp.arange(NTYPES, dtype=jnp.int32)[None, :]).astype(F32)
    types = jnp.dot(selector, type_table.astype(F32), precision=lax.Precision.HIGHEST)
    types = jnp.tile(types, (128 // cols, 1))
    first = (lax.axis_index("rows") > 0).astype(F32)
    valid = jnp.broadcast_to(jnp.stack([jnp.sum(validity), first])[:, None], (2, 128))
    cell_table = table.reshape(cells, width)
    cot = out_cotangent.reshape(cells, width)

    row_norm, row_qkv, row_mixed, after_rows, col_norm, col_qkv, edge = call(
        first_kernel,
        [((cells, width), BF16), ((cells, 3 * width), BF16), ((cells, width), BF16), ((cells, width), F32),
         ((cells, width), BF16), ((cells, 3 * width), F32), ((half * cols, 2 * width), BF16)],
        [], cell_table, types, row_inputs, row_merge, column_inputs,
    )
    halo = from_behind(edge, "rows", 1)
    lanes = width // 128
    col_mixed, after_columns, summary, summary_norm, squery, skv = call(
        second_kernel,
        [((cells, width), BF16), ((cells, width), F32), ((cols, width), F32), ((cols, width), BF16),
         ((cols, width), BF16), ((cols, 2 * width), BF16)],
        [((3 * lanes, cells, 128), F32), ((2 * lanes, half * cols, 128), F32), ((lanes, cells, 128), F32)],
        after_rows, col_qkv, halo, valid, column_merge, summary_queries, summary_pairs,
    )
    n = lax.axis_size("rows")
    (every_pair,) = gather(n, 0, skv)
    encoded, col_grad, query_grad, query_and_grad, lines, packed3 = call(
        partial(third_kernel, scale),
        [((cells, width), BF16), ((cells, width), F32), ((cols, width), BF16), ((cols, 2 * width), BF16),
         ((8, HEADS * cols), F32), ((5, width, width), BF16)],
        [((cols, width), F32), ((cells, hidden), BF16), ((cells, width), BF16), ((cells, hidden), BF16)],
        after_columns, squery, every_pair, cot, summary_merge, expand_weight, reduce_weight,
    )
    every_query, every_line = gather(n, 1, query_and_grad, lines)
    d_after, dqkv, halo_grad, packed4 = call(
        partial(fourth_kernel, scale),
        [((cells, width), F32), ((cells, 3 * width), F32), ((half * cols, 2 * width), BF16), ((4, width, width), BF16)],
        [((3 * lanes, cells, 128), F32), ((2 * lanes, half * cols, 128), F32), ((lanes, cells, 128), F32),
         ((3 * lanes, cells, 128), F32), ((2 * lanes, half * cols, 128), F32), ((cells, width), BF16)],
        col_grad, query_grad, every_query, every_line, skv, summary, summary_norm, col_qkv, halo, valid,
        col_mixed, column_merge, summary_queries, summary_pairs,
    )
    edge_grad = from_behind(halo_grad, "rows", -1)
    table_grad, type_sum, packed5 = call(
        partial(fifth_kernel, scale),
        [((cells, width), BF16), ((cols, width), F32), ((7, width, width), BF16)],
        [((cells, 3 * width), BF16), ((cells, width), BF16), ((cells, 3 * width), BF16)],
        dqkv, edge_grad, d_after, after_rows, cell_table, types, row_norm, row_qkv, row_mixed, col_norm,
        row_inputs, row_merge, column_inputs,
    )
    if n == 16:
        packed = reduce_all(packed3, packed4, packed5, type_sum)
    else:
        blocks = jnp.concatenate([packed3, packed4, packed5], axis=0)
        extra = jnp.broadcast_to(type_sum.astype(BF16)[:, None], (cols, 16, width))
        packed = lax.psum(jnp.concatenate([blocks, extra], axis=1), "rows")
    totals = call(
        unpack_kernel,
        [((NTYPES, width), F32), ((width, 3 * width), F32), ((width, width), F32), ((width, 3 * width), F32),
         ((width, width), F32), ((width, width), F32), ((width, 2 * width), F32), ((width, width), F32),
         ((width, hidden), F32), ((hidden, width), F32)],
        [], packed, selector.astype(BF16),
    )
    return (encoded.reshape(table.shape), table_grad.reshape(table.shape)) + tuple(totals)


def solution(mesh):
    split = P(("win", "rows"), None, None)
    return jax.shard_map(
        shards,
        mesh=mesh,
        in_specs=(split, P(("win", "rows")), P("win")) + (P(),) * 10 + (split,),
        out_specs=(split, split) + (P("win", None),) * 10,
        check_vma=False,
    )
```

```python
from functools import partial
import math

import jax
import jax.numpy as jnp
from jax import lax
from jax.experimental import pallas as pl
from jax.experimental.pallas import tpu as pltpu
from jax.sharding import PartitionSpec as P

HEADS = 8
NTYPES = 8
SPAN = 64
EPSILON = 1e-05
F32 = jnp.float32
BF16 = jnp.bfloat16
VMEM_LIMIT = 56 * 1024 * 1024


def from_behind(block, axis, distance):
    devices = range(lax.axis_size(axis))
    route = [(i - distance, i) for i in devices if i - distance in devices]
    return lax.ppermute(block, axis, route)


def dot_nn(a, b):
    return lax.dot_general(a, b, (((1,), (0,)), ((), ())), preferred_element_type=F32)


def dot_nt(a, b):
    return lax.dot_general(a, b, (((1,), (1,)), ((), ())), preferred_element_type=F32)


def dot_tn(a, b):
    return lax.dot_general(a, b, (((0,), (0,)), ((), ())), preferred_element_type=F32)


def norm(x):
    center = x - jnp.mean(x, axis=-1, keepdims=True)
    scale = lax.rsqrt(jnp.mean(center * center, axis=-1, keepdims=True) + EPSILON)
    return center * scale, scale


def norm_back(grad, hat, scale):
    first = jnp.mean(grad, axis=-1, keepdims=True)
    second = jnp.mean(grad * hat, axis=-1, keepdims=True)
    return scale * (grad - first - hat * second)


def stack_heads(x):
    head = lax.broadcasted_iota(jnp.int32, (1, x.shape[1]), 1) // (x.shape[1] // HEADS)
    return jnp.concatenate([x * (head == h).astype(F32).astype(BF16) for h in range(HEADS)], axis=0)


def merge_heads(x):
    n = x.shape[0] // HEADS
    head = lax.broadcasted_iota(jnp.int32, (n, x.shape[1]), 1) // (x.shape[1] // HEADS)
    out = x[:n]
    for h in range(1, HEADS):
        out = jnp.where(head == h, x[h * n : (h + 1) * n], out)
    return out


def shares_of(stacked, keys, allowed):
    width = keys.shape[1] // HEADS
    scores = jnp.exp2(dot_nt(keys, stacked) * (math.log2(math.e) / math.sqrt(width)))
    if allowed is not None:
        scores = jnp.where(allowed, scores, 0.0)
    total = jnp.sum(scores, axis=0, keepdims=True)
    return scores / total, total


def attend(query, keys, values, allowed):
    shares = shares_of(stack_heads(query), keys, allowed)[0].astype(BF16)
    return merge_heads(dot_tn(shares, values)).astype(BF16)


def attend_back(query, keys, values, grad, allowed):
    width = keys.shape[1] // HEADS
    stacked = stack_heads(query)
    grads = stack_heads(grad)
    shares = shares_of(stacked, keys, allowed)[0]
    share_grad = dot_nt(values, grads)
    total = jnp.sum(share_grad * shares, axis=0, keepdims=True)
    score_grad = (shares * (share_grad - total) * (1.0 / math.sqrt(width))).astype(BF16)
    query_grad = merge_heads(dot_tn(score_grad, keys))
    key_grad = dot_nn(score_grad, stacked)
    value_grad = dot_nn(shares.astype(BF16), grads)
    return query_grad, key_grad, value_grad


def query_back(query, keys, values, grad):
    width = keys.shape[1] // HEADS
    shares, norms = shares_of(stack_heads(query), keys, None)
    share_grad = dot_nt(values, stack_heads(grad))
    total = jnp.sum(share_grad * shares, axis=0, keepdims=True)
    score_grad = (shares * (share_grad - total) * (1.0 / math.sqrt(width))).astype(BF16)
    return merge_heads(dot_tn(score_grad, keys)), norms, total


def pair_back(queries, grads, lines, keys, values):
    width = keys.shape[1] // HEADS
    n = queries.shape[0]
    stacked = jnp.concatenate([stack_heads(queries[i]) for i in range(n)], axis=0)
    stacked_grads = jnp.concatenate([stack_heads(grads[i]) for i in range(n)], axis=0)
    norms = jnp.concatenate([lines[i][0:1] for i in range(n)], axis=1)
    total = jnp.concatenate([lines[i][1:2] for i in range(n)], axis=1)
    shares = jnp.exp2(dot_nt(keys, stacked) * (math.log2(math.e) / math.sqrt(width))) / norms
    share_grad = dot_nt(values, stacked_grads)
    score_grad = (shares * (share_grad - total) * (1.0 / math.sqrt(width))).astype(BF16)
    return dot_nn(score_grad, stacked), dot_nn(shares.astype(BF16), stacked_grads)


def row_allowed(cells, cols):
    key = lax.broadcasted_iota(jnp.int32, (cells, HEADS * cells), 0)
    query = lax.broadcasted_iota(jnp.int32, (cells, HEADS * cells), 1)
    return key // cols == (query % cells) // cols


def column_allowed(rows, valid):
    half = rows // 2
    shape = (rows + half, HEADS * rows)
    key = lax.broadcasted_iota(jnp.int32, shape, 0)
    start = (lax.broadcasted_iota(jnp.int32, shape, 1) % rows) // half * half
    spot = (key - half).astype(F32)
    present = (spot < valid[0:1, 0:1]) & (spot >= -half * valid[1:2, 0:1])
    return (key >= start) & (key < start + rows) & present


def cell_weights(start, count, cols, valid):
    row = (start + lax.broadcasted_iota(jnp.int32, (count, 1), 0)) // cols
    total = valid[0:1, 0:1]
    return jnp.where(row.astype(F32) < total, 1.0 / total, 0.0)


def first_kernel(table, types, row_in, row_merge, col_in, row_norm, row_qkv, row_mixed, after_rows, col_norm, col_qkv, edge):
    cells = types.shape[0]
    width = types.shape[1]
    groups = table.shape[0] // cells
    allowed = row_allowed(cells, 16)

    def step(g, _):
        at = pl.ds(pl.multiple_of(g * cells, cells), cells)
        residual = table[at, :].astype(F32) + types[...]
        normed = norm(residual)[0].astype(BF16)
        row_norm[at, :] = normed
        qkv = dot_nn(normed, row_in[...]).astype(BF16)
        row_qkv[at, :] = qkv
        mixed = attend(qkv[:, :width], qkv[:, width : 2 * width], qkv[:, 2 * width :], allowed)
        row_mixed[at, :] = mixed
        after = residual + dot_nn(mixed, row_merge[...])
        after_rows[at, :] = after
        cnormed = norm(after)[0].astype(BF16)
        col_norm[at, :] = cnormed
        cqkv = dot_nn(cnormed, col_in[...]).astype(BF16)
        col_qkv[at, :] = cqkv.astype(F32)

        return 0

    lax.fori_loop(0, groups, step, 0, unroll=4)
    edge[...] = col_qkv[table.shape[0] // 2 :, width:].astype(BF16)


def column_parts(cqkv, halo, column, rows, cols, width):
    here = pl.ds(column, rows, stride=cols)
    before = pl.ds(column, rows // 2, stride=cols)
    parts = []
    for i in range(width // 128 * 3):
        parts.append(cqkv[i][here, :].astype(BF16))
    halos = [halo[i][before, :].astype(BF16) for i in range(width // 128 * 2)]
    per = width // 128
    query = jnp.concatenate(parts[:per], axis=1)
    keys = jnp.concatenate([jnp.concatenate(halos[:per], axis=1), jnp.concatenate(parts[per : 2 * per], axis=1)], axis=0)
    values = jnp.concatenate([jnp.concatenate(halos[per:], axis=1), jnp.concatenate(parts[2 * per :], axis=1)], axis=0)
    return query, keys, values


def spread(src, dst):
    for i in range(dst.shape[0]):
        dst[i] = src[:, i * 128 : (i + 1) * 128].astype(F32)


def second_kernel(after_rows, cqkv, halo, valid, col_merge, squeries, spairs, col_mixed, after_columns, summary, summary_norm, squery, skv, cqkv_s, halo_s, mixed_s):
    cells, width = after_rows.shape
    rows = SPAN
    cols = cells // rows
    spread(cqkv, cqkv_s)
    spread(halo, halo_s)
    allowed = column_allowed(rows, valid)

    def step(c, _):
        query, keys, values = column_parts([cqkv_s.at[i] for i in range(6)], [halo_s.at[i] for i in range(4)], c, rows, cols, width)
        mixed = attend(query, keys, values, allowed).astype(F32)
        for i in range(width // 128):
            mixed_s.at[i][pl.ds(c, rows, stride=cols), :] = mixed[:, i * 128 : (i + 1) * 128]
        return 0

    lax.fori_loop(0, cols, step, 0, unroll=4)
    chunk = 128
    summary[...] = jnp.zeros_like(summary)

    def merge(g, _):
        at = pl.ds(pl.multiple_of(g * chunk, chunk), chunk)
        mixed = jnp.concatenate([mixed_s.at[i][at, :] for i in range(width // 128)], axis=1).astype(BF16)
        col_mixed[at, :] = mixed
        after = after_rows[at, :] + dot_nn(mixed, col_merge[...])
        after_columns[at, :] = after
        weighted = after * cell_weights(g * chunk, chunk, cols, valid)
        summary[...] += jnp.sum(weighted.reshape(chunk // cols, cols, width), axis=0)
        return 0

    lax.fori_loop(0, cells // chunk, merge, 0, unroll=4)
    normed = norm(summary[...])[0].astype(BF16)
    summary_norm[...] = normed
    squery[...] = dot_nn(normed, squeries[...]).astype(BF16)
    skv[...] = dot_nn(normed, spairs[...]).astype(BF16)


def gelu_parts(x):
    k = math.sqrt(2.0 / math.pi)
    t = jnp.tanh(k * (x + 0.044715 * x * x * x))
    value = 0.5 * x * (1.0 + t)
    slope = 0.5 * (1.0 + t) + 0.5 * x * (1.0 - t * t) * (k * (1.0 + 3 * 0.044715 * x * x))
    return value, slope


def third_kernel(scale, after_columns, squery, pairs, cot, smerge, expand, reduce, encoded, col_grad, query_grad, query_and_grad, lines, packed, span_s, hidden_s, feed_s, du_s):
    cells, width = after_columns.shape
    cols = squery.shape[0]
    query = squery[...]
    tokens = pairs.shape[0] * cols
    keys = pairs[:, :, :width].reshape(tokens, width)
    values = pairs[:, :, width:].reshape(tokens, width)
    mixed = attend(query, keys, values, None)
    chunk = 128
    term = jnp.concatenate([dot_nn(mixed, smerge[...])] * (chunk // cols), axis=0)
    span_s[...] = jnp.zeros_like(span_s)

    def step(g, _):
        at = pl.ds(pl.multiple_of(g * chunk, chunk), chunk)
        mixed_in = after_columns[at, :] + term
        hat, inv = norm(mixed_in)
        feed = hat.astype(BF16)
        value, slope = gelu_parts(dot_nn(feed, expand[...]))
        hidden = value.astype(BF16)
        encoded[at, :] = (mixed_in + dot_nn(hidden, reduce[...])).astype(BF16)
        g_out = cot[at, :]
        d_up = (dot_nt(g_out, reduce[...]) * slope).astype(BF16)
        d_feed = dot_nt(d_up, expand[...])
        d_in = g_out.astype(F32) + norm_back(d_feed, hat, inv)
        col_grad[at, :] = d_in
        span_s[...] += jnp.sum(d_in.reshape(chunk // cols, cols, width), axis=0)
        hidden_s[at, :] = hidden
        feed_s[at, :] = feed
        du_s[at, :] = d_up
        return 0

    lax.fori_loop(0, cells // chunk, step, 0, unroll=4)
    d_span = span_s[...].astype(BF16)
    packed[0] = (dot_tn(mixed, d_span) * scale).astype(BF16)
    d_mixed = dot_nt(d_span, smerge[...]).astype(BF16)
    dq, norms, total = query_back(query, keys, values, d_mixed)
    query_grad[...] = dq.astype(BF16)
    query_and_grad[:, :width] = query
    query_and_grad[:, width:] = d_mixed
    lines[...] = jnp.concatenate([norms, total, jnp.zeros((6, norms.shape[1]), F32)], axis=0)
    expand_g = (dot_tn(feed_s[...], du_s[...]) * scale).astype(BF16)
    reduce_g = (dot_tn(hidden_s[...], cot[...]) * scale).astype(BF16)
    for i in range(2):
        packed[1 + i] = expand_g[:, i * width : (i + 1) * width]
        packed[3 + i] = reduce_g[i * width : (i + 1) * width, :]


def fourth_kernel(scale, col_grad, query_grad, every_query, every_line, skv, summary, summary_norm, cqkv, halo, valid, col_mixed, col_merge, squeries, spairs, d_after, dqkv, halo_grad, packed, cqkv_s, halo_s, dmix_s, dqkv_s, dhalo_s, dab_s):
    cells, width = col_grad.shape
    rows = SPAN
    cols = cells // rows
    spread(cqkv, cqkv_s)
    spread(halo, halo_s)
    qg = query_grad[...]
    dk, dv = pair_back(every_query[:, :, :width], every_query[:, :, width:], every_line[...], skv[:, :width], skv[:, width:])
    pg = jnp.concatenate([dk.astype(BF16), dv.astype(BF16)], axis=1)
    packed[1] = (dot_tn(summary_norm[...], qg) * scale).astype(BF16)
    pairs_g = (dot_tn(summary_norm[...], pg) * scale).astype(BF16)
    for i in range(2):
        packed[2 + i] = pairs_g[:, i * width : (i + 1) * width]
    d_norm = dot_nt(qg, squeries[...]) + dot_nt(pg, spairs[...])
    hat, inv = norm(summary[...])
    chunk = 128
    d_summary = jnp.concatenate([norm_back(d_norm, hat, inv)] * (chunk // cols), axis=0)

    def before(g, _):
        at = pl.ds(pl.multiple_of(g * chunk, chunk), chunk)
        grad = col_grad[at, :] + d_summary * cell_weights(g * chunk, chunk, cols, valid)
        d_after[at, :] = grad
        rounded = grad.astype(BF16)
        dab_s[at, :] = rounded
        d_mixed = dot_nt(rounded, col_merge[...])
        for i in range(width // 128):
            dmix_s.at[i][at, :] = d_mixed[:, i * 128 : (i + 1) * 128]
        return 0

    lax.fori_loop(0, cells // chunk, before, 0, unroll=4)
    packed[0] = (dot_tn(col_mixed[...], dab_s[...]) * scale).astype(BF16)
    allowed = column_allowed(rows, valid)
    half = rows // 2
    per = width // 128

    def step(c, _):
        query, keys, values = column_parts([cqkv_s.at[i] for i in range(6)], [halo_s.at[i] for i in range(4)], c, rows, cols, width)
        here = pl.ds(c, rows, stride=cols)
        behind = pl.ds(c, half, stride=cols)
        grad = jnp.concatenate([dmix_s.at[i][here, :].astype(BF16) for i in range(per)], axis=1)
        dq, dk, dv = attend_back(query, keys, values, grad, allowed)
        for i in range(per):
            lanes = slice(i * 128, (i + 1) * 128)
            dqkv_s.at[i][here, :] = dq[:, lanes]
            dqkv_s.at[per + i][here, :] = dk[half:, lanes]
            dqkv_s.at[2 * per + i][here, :] = dv[half:, lanes]
            dhalo_s.at[i][behind, :] = dk[:half, lanes]
            dhalo_s.at[per + i][behind, :] = dv[:half, lanes]
        return 0

    lax.fori_loop(0, cols, step, 0, unroll=4)
    for i in range(3 * per):
        dqkv[:, i * 128 : (i + 1) * 128] = dqkv_s[i]
    for i in range(2 * per):
        halo_grad[:, i * 128 : (i + 1) * 128] = dhalo_s[i].astype(BF16)


def fifth_kernel(scale, dcol, edge_grad, d_after_in, after_rows, table, types, row_norm, row_qkv, row_mixed, col_norm, row_in, row_merge, col_in, table_grad, type_sum, packed, dcol_s, dab_s, drow_s):
    cells = types.shape[0]
    width = types.shape[1]
    groups = table.shape[0] // cells
    cols = type_sum.shape[0]
    allowed = row_allowed(cells, cols)
    type_sum[...] = jnp.zeros_like(type_sum)

    def step(g, _):
        at = pl.ds(pl.multiple_of(g * cells, cells), cells)
        late = (g >= groups // 2).astype(F32)
        edge_at = pl.ds(pl.multiple_of(jnp.maximum(g - groups // 2, 0) * cells, cells), cells)
        edge = edge_grad[edge_at, :].astype(F32) * late
        d_query = dcol[at, :width].astype(BF16)
        d_pairs = (dcol[at, width:] + edge).astype(BF16)
        d_qkv = jnp.concatenate([d_query, d_pairs], axis=1)
        dcol_s[at, :] = d_qkv
        hat, inv = norm(after_rows[at, :])
        d_after = d_after_in[at, :] + norm_back(dot_nt(d_qkv, col_in[...]), hat, inv)
        rounded = d_after.astype(BF16)
        dab_s[at, :] = rounded
        d_mixed = dot_nt(rounded, row_merge[...]).astype(BF16)
        qkv = row_qkv[at, :]
        dq, dk, dv = attend_back(qkv[:, :width], qkv[:, width : 2 * width], qkv[:, 2 * width :], d_mixed, allowed)
        d_row = jnp.concatenate([dq.astype(BF16), dk.astype(BF16), dv.astype(BF16)], axis=1)
        drow_s[at, :] = d_row
        hat, inv = norm(table[at, :].astype(F32) + types[...])
        d_res = d_after + norm_back(dot_nt(d_row, row_in[...]), hat, inv)
        table_grad[at, :] = d_res.astype(BF16)
        type_sum[...] += jnp.sum(d_res.reshape(cells // cols, cols, width), axis=0)
        return 0

    lax.fori_loop(0, groups, step, 0, unroll=4)
    col_in_g = (dot_tn(col_norm[...], dcol_s[...]) * scale).astype(BF16)
    row_in_g = (dot_tn(row_norm[...], drow_s[...]) * scale).astype(BF16)
    for i in range(3):
        packed[i] = row_in_g[:, i * width : (i + 1) * width]
        packed[3 + i] = col_in_g[:, i * width : (i + 1) * width]
    packed[6] = (dot_tn(row_mixed[...], dab_s[...]) * scale).astype(BF16)
    type_sum[...] = type_sum[...] * scale


def greet(peers):
    barrier = pltpu.get_barrier_semaphore()
    for peer in peers:
        pl.semaphore_signal(barrier, inc=1, device_id={"rows": peer}, device_id_type=pl.DeviceIdType.MESH)
    pl.semaphore_wait(barrier, len(peers))


def push(src, dst, send, recv, peer):
    copy = pltpu.make_async_remote_copy(
        src_ref=src, dst_ref=dst, send_sem=send, recv_sem=recv,
        device_id={"rows": peer}, device_id_type=pl.DeviceIdType.MESH,
    )
    copy.start()
    return copy


def gather_kernel(n, count, *refs):
    blocks, outs, holds, (send, recv) = refs[:count], refs[count : 2 * count], refs[2 * count : 3 * count], refs[3 * count :]
    me = lax.axis_index("rows")
    peers = [lax.rem(me + d, n) for d in range(1, n)]
    greet(peers)
    copies = []
    for d in range(n - 1):
        for i in range(count):
            copies.append(push(blocks[i], holds[i].at[me], send.at[i, d], recv.at[i, d], peers[d]))
    for i in range(count):
        holds[i][pl.ds(me, 1)] = blocks[i][...][None]
    for copy in copies:
        copy.wait()
    for i in range(count):
        outs[i][...] = holds[i][...]


def gather(n, identity, *blocks):
    vmem = pl.BlockSpec(memory_space=pltpu.VMEM)
    count = len(blocks)
    return pl.pallas_call(
        partial(gather_kernel, n, count),
        out_shape=[jax.ShapeDtypeStruct((n,) + x.shape, x.dtype) for x in blocks],
        in_specs=[vmem] * count,
        out_specs=[vmem] * count,
        scratch_shapes=[pltpu.VMEM((n,) + x.shape, x.dtype) for x in blocks]
        + [pltpu.SemaphoreType.DMA((count, n - 1)), pltpu.SemaphoreType.DMA((count, n - 1))],
        compiler_params=pltpu.CompilerParams(collective_id=identity, has_side_effects=True),
    )(*blocks)


def reduce_kernel(g3, g4, g5, sums, out, held, from_core, from_x, from_z, whole, send, recv):
    me = lax.axis_index("rows")
    core = lax.rem(me, 2)
    x = lax.rem(me // 2, 2)
    z = me // 4
    by_core = me + 1 - 2 * core
    by_x = me + 2 - 4 * x
    zs = [lax.rem(z + d, 4) for d in range(1, 4)]
    by_z = [other * 4 + x * 2 + core for other in zs]
    greet([by_core, by_x] + by_z)
    rows = g3.shape[1]
    index = 0
    for part in (g3, g4, g5):
        for i in range(part.shape[0]):
            held[index, :rows, :] = part[i]
            index += 1
    for i in range(16):
        held[i, rows:, :] = jnp.broadcast_to(sums[i : i + 1, :], (16, sums.shape[1])).astype(BF16)

    base = core * 8 + x * 4
    mine = base + z
    tall = rows + 16
    cuts = [0, tall - 3 * (rows // 4)] + [tall - k * (rows // 4) for k in (2, 1, 0)]
    chunks = [slice(cuts[c], cuts[c + 1]) for c in range(4)]
    sizes = [cuts[c + 1] - cuts[c] for c in range(4)]
    flying = {}

    def part(ref, c, at):
        return ref.at[at, pl.ds(cuts[c], sizes[c])]

    def finish(c):
        for copy in flying.pop(c):
            copy.wait()

    def core_out(c):
        at = pl.ds((1 - core) * 8, 8)
        flying[c] = [push(part(held, c, at), part(from_core, c, pl.ds(0, 8)), send.at[0, c], recv.at[0, c], by_core)]

    def x_out(c):
        finish(c)
        for i in range(8):
            total = held[core * 8 + i, chunks[c], :].astype(F32) + from_core[i, chunks[c], :].astype(F32)
            held[core * 8 + i, chunks[c], :] = total.astype(BF16)
        at = pl.ds(core * 8 + (1 - x) * 4, 4)
        flying[c] = [push(part(held, c, at), part(from_x, c, pl.ds(0, 4)), send.at[1, c], recv.at[1, c], by_x)]

    def z_out(c):
        finish(c)
        for i in range(4):
            total = held[base + i, chunks[c], :].astype(F32) + from_x[i, chunks[c], :].astype(F32)
            held[base + i, chunks[c], :] = total.astype(BF16)
        flying[c] = [
            push(part(held, c, base + zs[d]), part(from_z, c, d), send.at[2 + d, c], recv.at[2 + d, c], by_z[d])
            for d in range(3)
        ]

    def z_back(c):
        finish(c)
        total = held[mine, chunks[c], :].astype(F32)
        for d in range(3):
            total = total + from_z[d, chunks[c], :].astype(F32)
        whole[mine, chunks[c], :] = total.astype(BF16)
        flying[c] = [
            push(part(whole, c, mine), part(whole, c, mine), send.at[5 + d, c], recv.at[5 + d, c], by_z[d]) for d in range(3)
        ]

    def x_back(c):
        finish(c)
        at = pl.ds(base, 4)
        flying[c] = [push(part(whole, c, at), part(whole, c, at), send.at[8, c], recv.at[8, c], by_x)]

    def core_back(c):
        finish(c)
        at = pl.ds(core * 8, 8)
        flying[c] = [push(part(whole, c, at), part(whole, c, at), send.at[9, c], recv.at[9, c], by_core)]

    stages = [core_out, x_out, z_out, z_back, x_back, core_back, finish]
    for tick in range(4 + len(stages) - 1):
        for number in reversed(range(len(stages))):
            if 0 <= tick - number < 4:
                stages[number](tick - number)
    out[...] = whole[...]


def reduce_all(g3, g4, g5, sums):
    tall, width = g3.shape[1] + 16, g3.shape[2]
    vmem = pl.BlockSpec(memory_space=pltpu.VMEM)
    return pl.pallas_call(
        reduce_kernel,
        out_shape=jax.ShapeDtypeStruct((16, tall, width), BF16),
        in_specs=[vmem] * 4,
        out_specs=vmem,
        scratch_shapes=[pltpu.VMEM((count, tall, width), BF16) for count in (16, 8, 4, 3, 16)]
        + [pltpu.SemaphoreType.DMA((10, 4)), pltpu.SemaphoreType.DMA((10, 4))],
        compiler_params=pltpu.CompilerParams(collective_id=2, has_side_effects=True, vmem_limit_bytes=VMEM_LIMIT),
    )(g3, g4, g5, sums)


def unpack_kernel(packed, select, type_g, row_in_g, row_merge_g, col_in_g, cmerge_g, queries_g, pairs_g, smerge_g, expand_g, reduce_g):
    rows, width = cmerge_g.shape
    sums = jnp.concatenate([packed[i, rows:, :].astype(F32)[:1] for i in range(16)], axis=0).astype(BF16)
    type_g[...] = dot_tn(select[...], sums)

    def wide(out, start, count):
        for i in range(count):
            out[:, i * width : (i + 1) * width] = packed[start + i, :rows, :].astype(F32)

    wide(smerge_g, 0, 1)
    wide(expand_g, 1, 2)
    for i in range(2):
        reduce_g[i * rows : (i + 1) * rows, :] = packed[3 + i, :rows, :].astype(F32)
    wide(cmerge_g, 5, 1)
    wide(queries_g, 6, 1)
    wide(pairs_g, 7, 2)
    wide(row_in_g, 9, 3)
    wide(col_in_g, 12, 3)
    wide(row_merge_g, 15, 1)


def call(body, outs, scratch, *args):
    return pl.pallas_call(
        body,
        out_shape=[jax.ShapeDtypeStruct(shape, kind) for shape, kind in outs],
        scratch_shapes=[pltpu.VMEM(shape, kind) for shape, kind in scratch],
        compiler_params=pltpu.CompilerParams(vmem_limit_bytes=VMEM_LIMIT),
    )(*args)


def shards(
    table, row_mask, column_types, type_table, row_inputs, row_merge, column_inputs, column_merge,
    summary_queries, summary_pairs, summary_merge, expand_weight, reduce_weight, out_cotangent,
):
    rows, cols, width = table.shape
    cells = rows * cols
    half = rows // 2
    hidden = expand_weight.shape[1]
    scale = 1.0 / math.sqrt(rows * lax.axis_size("rows") * cols)
    validity = row_mask.astype(F32)
    selector = (column_types[:, None] == jnp.arange(NTYPES, dtype=jnp.int32)[None, :]).astype(F32)
    types = jnp.dot(selector, type_table.astype(F32), precision=lax.Precision.HIGHEST)
    types = jnp.tile(types, (128 // cols, 1))
    first = (lax.axis_index("rows") > 0).astype(F32)
    valid = jnp.broadcast_to(jnp.stack([jnp.sum(validity), first])[:, None], (2, 128))
    cell_table = table.reshape(cells, width)
    cot = out_cotangent.reshape(cells, width)

    row_norm, row_qkv, row_mixed, after_rows, col_norm, col_qkv, edge = call(
        first_kernel,
        [((cells, width), BF16), ((cells, 3 * width), BF16), ((cells, width), BF16), ((cells, width), F32),
         ((cells, width), BF16), ((cells, 3 * width), F32), ((half * cols, 2 * width), BF16)],
        [], cell_table, types, row_inputs, row_merge, column_inputs,
    )
    halo = from_behind(edge, "rows", 1)
    lanes = width // 128
    col_mixed, after_columns, summary, summary_norm, squery, skv = call(
        second_kernel,
        [((cells, width), BF16), ((cells, width), F32), ((cols, width), F32), ((cols, width), BF16),
         ((cols, width), BF16), ((cols, 2 * width), BF16)],
        [((3 * lanes, cells, 128), F32), ((2 * lanes, half * cols, 128), F32), ((lanes, cells, 128), F32)],
        after_rows, col_qkv, halo, valid, column_merge, summary_queries, summary_pairs,
    )
    n = lax.axis_size("rows")
    (every_pair,) = gather(n, 0, skv)
    encoded, col_grad, query_grad, query_and_grad, lines, packed3 = call(
        partial(third_kernel, scale),
        [((cells, width), BF16), ((cells, width), F32), ((cols, width), BF16), ((cols, 2 * width), BF16),
         ((8, HEADS * cols), F32), ((5, width, width), BF16)],
        [((cols, width), F32), ((cells, hidden), BF16), ((cells, width), BF16), ((cells, hidden), BF16)],
        after_columns, squery, every_pair, cot, summary_merge, expand_weight, reduce_weight,
    )
    every_query, every_line = gather(n, 1, query_and_grad, lines)
    d_after, dqkv, halo_grad, packed4 = call(
        partial(fourth_kernel, scale),
        [((cells, width), F32), ((cells, 3 * width), F32), ((half * cols, 2 * width), BF16), ((4, width, width), BF16)],
        [((3 * lanes, cells, 128), F32), ((2 * lanes, half * cols, 128), F32), ((lanes, cells, 128), F32),
         ((3 * lanes, cells, 128), F32), ((2 * lanes, half * cols, 128), F32), ((cells, width), BF16)],
        col_grad, query_grad, every_query, every_line, skv, summary, summary_norm, col_qkv, halo, valid,
        col_mixed, column_merge, summary_queries, summary_pairs,
    )
    edge_grad = from_behind(halo_grad, "rows", -1)
    table_grad, type_sum, packed5 = call(
        partial(fifth_kernel, scale),
        [((cells, width), BF16), ((cols, width), F32), ((7, width, width), BF16)],
        [((cells, 3 * width), BF16), ((cells, width), BF16), ((cells, 3 * width), BF16)],
        dqkv, edge_grad, d_after, after_rows, cell_table, types, row_norm, row_qkv, row_mixed, col_norm,
        row_inputs, row_merge, column_inputs,
    )
    if n == 16:
        packed = reduce_all(packed3, packed4, packed5, type_sum)
    else:
        blocks = jnp.concatenate([packed3, packed4, packed5], axis=0)
        extra = jnp.broadcast_to(type_sum.astype(BF16)[:, None], (cols, 16, width))
        packed = lax.psum(jnp.concatenate([blocks, extra], axis=1), "rows")
    totals = call(
        unpack_kernel,
        [((NTYPES, width), F32), ((width, 3 * width), F32), ((width, width), F32), ((width, 3 * width), F32),
         ((width, width), F32), ((width, width), F32), ((width, 2 * width), F32), ((width, width), F32),
         ((width, hidden), F32), ((hidden, width), F32)],
        [], packed, selector.astype(BF16),
    )
    return (encoded.reshape(table.shape), table_grad.reshape(table.shape)) + tuple(totals)


def solution(mesh):
    split = P(("win", "rows"), None, None)
    return jax.shard_map(
        shards,
        mesh=mesh,
        in_specs=(split, P(("win", "rows")), P("win")) + (P(),) * 10 + (split,),
        out_specs=(split, split) + (P("win", None),) * 10,
        check_vma=False,
    )
```
